128 devices in a mesh: wide: 32 (over y, z, core), narrow: 4 (over x).
Axes of the slice: x: 4, y: 4, z: 4, core: 2. Of those that a mesh axis runs over, the one named last changes fastest.
Arguments:
- prefit_resid: float32 [5242880], P(('wide', 'narrow')), may hold values from -6 to 6
- source_partials: float32 [5, 5242880], P(None, ('wide', 'narrow')), may hold values from -6 to 6
- attitude_partials: float32 [4, 5242880], P(None, ('wide', 'narrow')), may hold values from -0.25 to 0.25
- spline_position: float32 [5242880], P(('wide', 'narrow')), may hold values from 0 to 1
- calib_partials: float32 [3, 5242880], P(None, ('wide', 'narrow')), may hold values from -2 to 2
- obs_source: int32 [5242880], P(('wide', 'narrow')), may hold values from 0 to 127
- block_count: int32 [8192], P(('wide', 'narrow')), may hold values from 320 to 640, as said below
- obs_range: int32 [5242880], P(('wide', 'narrow')), may hold values from 0 to 31, as said below
- obs_knot: int32 [5242880], P(('wide', 'narrow')), may hold values from 0 to 255
- obs_unit: int32 [5242880], P(('wide', 'narrow')), may hold values from 0 to 2015
- given_inverse: float32 [32, 1024, 1024], P('wide'), may hold values from -2.5 to 2.5, as said below
- knot_decay: float32 [4, 8192], P(None, 'wide'), may hold values from 0.15 to 1
Outputs:
- source_update: float32 [5, 1048576], P(None, ('wide', 'narrow'))
- attitude_update: float32 [4, 8192], P(None, 'wide')
- cal_update: float32 [3, 2016], P(None, 'narrow')
The draws below stay inside these ranges and needn't reach their ends.
Inputs may be any that keep to these rules, and one draw needn't show every extreme that they name: `block_count`: each block's live observations are its first slots; every device has one block with all 640 slots live. `obs_range`: at most 2560 of one device's observation slots fall in one time range; for each index along narrow, some time range holds exactly 2560 slots of every device of that index. `given_inverse`: each time range's given inverse is symmetric.
All inputs are finite; a program needn't handle non-finite values.
Results may differ from the reference program's by a relative error of at most 0.0003.
Values sent between devices are 32-bit elements; how exact they have to be, the bound alone decides.
No kernel may reach another device: no remote copies, remote signals or barrier semaphores. Data moves between devices by JAX's collectives and lax.ppermute only.
A program may use at most 64 MiB of HBM per device.

```python
import math
import jax
import jax.numpy as jnp
from jax import lax

SRC_BLK = 128
SLOT_BLK = 640
BLK_DEV = 64
KN_DEV = 256
RANGES = 32
GROUPS = 4
OBS_DEV = 40960
BLOCKS = 8192
SOURCES = 1048576
OBS_TOTAL = 5242880
CAP = 2560
ATTITUDE_KNOTS = 8192
CAL = 2016
DEVICES = 128


def draw_block_count(key, part):
    counts = jax.random.randint(jax.random.fold_in(key, 1), (DEVICES, BLK_DEV), SLOT_BLK // 2, SLOT_BLK + 1)
    chosen = jax.random.randint(jax.random.fold_in(key, 2), (DEVICES, 1), 0, BLK_DEV)
    counts = jnp.where(jnp.arange(BLK_DEV, dtype=jnp.int32)[None, :] == chosen, SLOT_BLK, counts)
    return counts.reshape(BLOCKS).astype(jnp.int32)


def draw_obs_range(key, part):
    root_random_key = jax.random.fold_in(key, 7)
    favoured = jax.random.randint(jax.random.fold_in(root_random_key, 1), (GROUPS,), 0, RANGES)
    others_total = OBS_DEV - CAP
    base_load = others_total // (RANGES - 1)
    remainder = others_total - base_load * (RANGES - 1)
    paired = (RANGES - 1) // 2

    def one_device(device_at):
        device_key = jax.random.fold_in(root_random_key, device_at + 100)
        heavy = favoured[device_at % GROUPS]
        others = (heavy + 1 + jax.random.permutation(jax.random.fold_in(device_key, 1), RANGES - 1)) % RANGES
        order_list = jnp.concatenate([heavy[None], others]).astype(jnp.int32)
        moved = jax.random.randint(jax.random.fold_in(device_key, 2), (max(paired, 1),), 0, base_load // 2 + 1)[:paired]
        loads = jnp.full((RANGES - 1,), base_load, jnp.int32)
        loads = loads.at[0:2 * paired:2].add(moved).at[1:2 * paired:2].add(-moved)
        loads = loads.at[0].add(remainder)
        bounds = jnp.cumsum(jnp.concatenate([jnp.array([CAP], jnp.int32), loads]))
        places = jax.random.permutation(jax.random.fold_in(device_key, 3), OBS_DEV)
        picked = jnp.searchsorted(bounds, places, side='right')
        return order_list[picked]
    return jax.vmap(one_device)(jnp.arange(DEVICES, dtype=jnp.int32)).reshape(OBS_TOTAL).astype(jnp.int32)


def draw_given_inverse(key, part):
    order_size = 4 * KN_DEV
    key_noise = jax.random.fold_in(key, 1)
    key_diag = jax.random.fold_in(key, 2)
    noise = jax.random.normal(key_noise, (RANGES, order_size, order_size), jnp.float32)
    diagonal = jax.random.uniform(key_diag, (RANGES, order_size), jnp.float32, 0.8, 2.4)
    off_part = (noise + jnp.swapaxes(noise, 1, 2)) * (0.45 / math.sqrt(2.0 * order_size))
    identity = jnp.eye(order_size, dtype=jnp.float32)
    return (off_part * (1.0 - identity) + diagonal[:, :, None] * identity).astype(jnp.float32)


def draw_knot_decay(key, part):
    share_slow = 0.5
    slow = jax.random.uniform(jax.random.fold_in(key, 1), (4, 1)) < share_slow
    fast_len = KN_DEV / 8.0 + (KN_DEV / 5.0 - KN_DEV / 8.0) * jax.random.uniform(jax.random.fold_in(key, 2), (4, 1))
    slow_rate = math.log(10.0) * jax.random.uniform(jax.random.fold_in(key, 3), (4, 1), jnp.float32, 0.03, 0.15) / ATTITUDE_KNOTS
    base_rate = jnp.where(slow, slow_rate, 1.0 / fast_len)
    rough = jax.random.uniform(jax.random.fold_in(key, 4), (4, ATTITUDE_KNOTS), jnp.float32, 0.5, 1.5)
    device_scale = jnp.repeat(jax.random.uniform(jax.random.fold_in(key, 5), (4, RANGES), jnp.float32, 1.0, 2.5), KN_DEV, axis=1)
    rates = base_rate * rough * device_scale
    multiplier = jax.random.uniform(jax.random.fold_in(key, 6), (4, ATTITUDE_KNOTS), jnp.float32, 0.5, 0.8)
    sudden_jump = jax.random.uniform(jax.random.fold_in(key, 7), (4, ATTITUDE_KNOTS)) < 3.0 / ATTITUDE_KNOTS
    retained_entries = jnp.exp(-rates)
    return jnp.where(sudden_jump, retained_entries * multiplier, retained_entries).astype(jnp.float32)


def draw_calib_partials(key, part):
    base_scale = math.sqrt(CAL / OBS_TOTAL) / 4.64
    spread = jnp.exp(math.log(10.0) * jax.random.uniform(jax.random.fold_in(key, 1), (1, OBS_TOTAL)))
    values = jnp.clip(jax.random.normal(jax.random.fold_in(key, 2), (3, OBS_TOTAL)), -5.0, 5.0)
    return (values * spread * base_scale).astype(jnp.float32)


def with_ends(values, stream_key, least, top_value):
    longest = values.shape.index(max(values.shape))
    spots = []
    for shift in (0, 1):
        where = [jax.random.randint(jax.random.fold_in(stream_key, axis), (), 0, length) for axis, length in enumerate(values.shape)]
        where[longest] = (where[longest] + shift) % values.shape[longest]
        spots.append(tuple(where))
    return values.at[spots[0]].set(least).at[spots[1]].set(top_value)


def levels(own_key, extent, split, low, largest):
    level, own = 1.0, jax.random.fold_in(own_key, 6)
    for axis_at, parts in split:
        draws = jnp.exp(jax.random.uniform(jax.random.fold_in(own, axis_at), (parts,), jnp.float32, low / len(split), largest / len(split)))
        level = level * jnp.repeat(draws, extent[axis_at] // parts).reshape([-1 if axis == axis_at else 1 for axis in range(len(extent))])
    return level


def scatter_about(stream_key, shape, width, reach, split=(), kind=jnp.bfloat16):
    loudness = levels(stream_key, shape, split, -0.22, 0.18) if split else 1.0
    drawn = jax.random.normal(stream_key, shape, jnp.float32) * width * loudness
    return jnp.minimum(jnp.maximum(drawn, -reach), reach).astype(kind)


def setup_inputs(seed: int = 0) -> dict:
    arg_keys = jax.random.split(jax.random.key(seed), 13)
    prefit_resid = scatter_about(arg_keys[0], (OBS_TOTAL,), 1.0, 6.0, ((0, 128),), jnp.float32)
    source_partials = scatter_about(arg_keys[1], (5, OBS_TOTAL), 1.0, 6.0, ((1, 128),), jnp.float32)
    attitude_partials = scatter_about(arg_keys[2], (4, OBS_TOTAL), (OBS_TOTAL // ATTITUDE_KNOTS) ** -0.5, 0.25, ((1, 128),), jnp.float32)
    spline_position = jnp.clip(1.0 * jax.random.uniform(arg_keys[3], (OBS_TOTAL,), jnp.float32) ** levels(arg_keys[3], (OBS_TOTAL,), ((0, 128),), -0.2, 0.2), 0.0, 1.0)
    calib_partials = draw_calib_partials(jax.random.fold_in(arg_keys[12], 71), 0)
    obs_source = with_ends(jax.random.randint(arg_keys[5], (OBS_TOTAL,), 0, SRC_BLK), jax.random.fold_in(arg_keys[5], 1), 0, SRC_BLK - 1).astype(jnp.int32)
    block_count = draw_block_count(jax.random.fold_in(arg_keys[12], 71), 0)
    obs_range = draw_obs_range(jax.random.fold_in(arg_keys[12], 71), 0)
    obs_knot = with_ends(jax.random.randint(arg_keys[8], (OBS_TOTAL,), 0, KN_DEV), jax.random.fold_in(arg_keys[8], 1), 0, KN_DEV - 1).astype(jnp.int32)
    obs_unit = with_ends(jax.random.randint(arg_keys[9], (OBS_TOTAL,), 0, CAL), jax.random.fold_in(arg_keys[9], 1), 0, CAL - 1).astype(jnp.int32)
    given_inverse = draw_given_inverse(jax.random.fold_in(arg_keys[12], 71), 0)
    knot_decay = draw_knot_decay(jax.random.fold_in(arg_keys[12], 71), 0)
    return {"prefit_resid": prefit_resid, "source_partials": source_partials, "attitude_partials": attitude_partials, "spline_position": spline_position, "calib_partials": calib_partials, "obs_source": obs_source, "block_count": block_count, "obs_range": obs_range, "obs_knot": obs_knot, "obs_unit": obs_unit, "given_inverse": given_inverse, "knot_decay": knot_decay}


source_pairs = [(left_at, right_at) for left_at in range(5) for right_at in range(left_at, 5)]
calib_pairs = [(left_at, right_at) for left_at in range(3) for right_at in range(left_at, 3)]

def spline(position):
    remain = 1.0 - position
    square_pos = position * position
    cube_pos = square_pos * position
    return jnp.stack([remain * remain * remain / 6.0, (3.0 * cube_pos - 6.0 * square_pos + 4.0) / 6.0, (-3.0 * cube_pos + 3.0 * square_pos + 3.0 * position + 1.0) / 6.0, cube_pos / 6.0])

def symmetric(values, pair_list, order_size):
    matrix = [[None] * order_size for index_lookup in range(order_size)]
    for slot_at, (left_at, right_at) in enumerate(pair_list):
        diag_add = 1.0 if left_at == right_at else 0.0
        entry_val = values[slot_at] + diag_add
        matrix[left_at][right_at] = entry_val
        matrix[right_at][left_at] = entry_val
    return matrix

def spd_solve(matrix, target):
    order_size = len(target)
    lower_tri = [[None] * order_size for index_lookup in range(order_size)]
    for column in range(order_size):
        pivot_sq = matrix[column][column]
        for before in range(column):
            pivot_sq = pivot_sq - lower_tri[column][before] * lower_tri[column][before]
        pivot_root = jnp.sqrt(pivot_sq)
        lower_tri[column][column] = pivot_root
        for row_at in range(column + 1, order_size):
            entry_val = matrix[row_at][column]
            for before in range(column):
                entry_val = entry_val - lower_tri[row_at][before] * lower_tri[column][before]
            lower_tri[row_at][column] = entry_val / pivot_root
    forward_sol = []
    for row_at in range(order_size):
        running = target[row_at]
        for before in range(row_at):
            running = running - lower_tri[row_at][before] * forward_sol[before]
        forward_sol.append(running / lower_tri[row_at][row_at])
    answer = [None] * order_size
    for row_at in reversed(range(order_size)):
        running = forward_sol[row_at]
        for before in range(row_at + 1, order_size):
            running = running - lower_tri[before][row_at] * answer[before]
        answer[row_at] = running / lower_tri[row_at][row_at]
    return answer

def reference(prefit_resid, source_partials, attitude_partials, spline_position, calib_partials, obs_source, block_count, obs_range, obs_knot, obs_unit, given_inverse, knot_decay):
    count_obs = prefit_resid.shape[0]
    slot_index = jnp.arange(count_obs, dtype=jnp.int32)
    block_index = slot_index // SLOT_BLK
    valid_mask = (slot_index % SLOT_BLK < block_count[block_index]).astype(jnp.float32)
    source_index = block_index * SRC_BLK + obs_source
    term_list = [source_partials[left_at] * source_partials[right_at] * valid_mask for left_at, right_at in source_pairs]
    term_list = term_list + [source_partials[param_at] * prefit_resid * valid_mask for param_at in range(5)]
    block_sums = [jax.ops.segment_sum(term_at, source_index, num_segments=SOURCES) for term_at in term_list]
    matrix = symmetric(block_sums[:15], source_pairs, 5)
    source_update = jnp.stack(spd_solve(matrix, block_sums[15:]))
    update_at_obs = source_update[:, source_index]
    resid_after = valid_mask * (prefit_resid - lax.optimization_barrier(jnp.sum(source_partials * update_at_obs, axis=0)))
    interval = obs_range * KN_DEV + obs_knot
    weights = spline(spline_position)
    columns = []
    for comp_at in range(4):
        line_sum = jnp.zeros((ATTITUDE_KNOTS + 3,), jnp.float32)
        for shift_at in range(4):
            line_sum = line_sum + jax.ops.segment_sum(weights[shift_at] * attitude_partials[comp_at] * resid_after, interval + shift_at, num_segments=ATTITUDE_KNOTS + 3)
        columns.append(line_sum[:ATTITUDE_KNOTS])
    att_rhs = jnp.stack(columns)
    span_rhs = att_rhs.reshape(4, RANGES, KN_DEV).transpose(1, 0, 2).reshape(RANGES, 4 * KN_DEV)
    solution_vector = jnp.einsum('rij,rj->ri', given_inverse, span_rhs, precision=lax.Precision.HIGHEST)
    solution_vector = solution_vector.reshape(RANGES, 4, KN_DEV).transpose(1, 0, 2).reshape(4, ATTITUDE_KNOTS)
    knot_gain = jnp.sqrt(1.0 - knot_decay * knot_decay)

    def advance(carried, inputs):
        rate_now, gain_now, value_now = inputs
        carried = rate_now * carried + gain_now * value_now
        return (carried, carried)
    final_state, history = lax.scan(advance, jnp.zeros((4,), jnp.float32), (knot_decay.T, knot_gain.T, solution_vector.T))
    attitude_update = history.T
    masked_cal = valid_mask * calib_partials
    cal_terms = [masked_cal[left_at] * masked_cal[right_at] for left_at, right_at in calib_pairs]
    cal_terms = cal_terms + [masked_cal[param_at] * resid_after for param_at in range(3)]
    cal_sums = [jax.ops.segment_sum(term_at, obs_unit, num_segments=CAL) for term_at in cal_terms]
    cal_matrix = symmetric(cal_sums[:6], calib_pairs, 3)
    cal_update = jnp.stack(spd_solve(cal_matrix, cal_sums[6:]))
    return (source_update, attitude_update, cal_update)
```

```python
import jax
import jax.numpy as jnp
from jax import lax
from jax.experimental import pallas as pl
from jax.experimental.pallas import tpu as pltpu
from jax.sharding import PartitionSpec as P

SRC_BLK = 128
SLOT_BLK = 640
CAL = 2016
GRP = 8
CHUNK = 1280
LANE = 128
ATT_BASE = 125
ATT_HI = 66
CAL_BASE = 252
CAL_HI = 8
F32 = jnp.float32
BF16 = jnp.bfloat16


def rounded(value):
    return value.astype(BF16).astype(F32)


def split3(value):
    top = rounded(value)
    rest = value - top
    mid = rounded(rest)
    return top, mid, rest - mid


def spd_solve(matrix, target):
    order = len(target)
    lower = [[None] * order for _ in range(order)]
    inv = [None] * order
    for col in range(order):
        pivot = matrix[col][col]
        for k in range(col):
            pivot = pivot - lower[col][k] * lower[col][k]
        inv[col] = 1.0 / jnp.sqrt(pivot)
        for row in range(col + 1, order):
            entry = matrix[row][col]
            for k in range(col):
                entry = entry - lower[row][k] * lower[col][k]
            lower[row][col] = entry * inv[col]
    forward = []
    for row in range(order):
        running = target[row]
        for k in range(row):
            running = running - lower[row][k] * forward[k]
        forward.append(running * inv[row])
    answer = [None] * order
    for row in reversed(range(order)):
        running = forward[row]
        for k in range(row + 1, order):
            running = running - lower[k][row] * answer[k]
        answer[row] = running * inv[row]
    return answer


NT = (((1,), (1,)), ((), ()))


def obs_kernel(
    count_ref, pre_ref, par_ref, att_ref, pos_ref, cal_ref, src_ref, rng_ref, knot_ref, unit_ref,
    upd_ref, att_out, cal_out,
    tile_s, hot_s, sums_s, upd_s, resid_s, unit_s, att_a, att_b, cal_a, cal_b, att_acc, cal_acc,
):
    step = pl.program_id(0)
    row8 = lax.broadcasted_iota(jnp.int32, (8, LANE), 0)
    row16 = lax.broadcasted_iota(jnp.int32, (16, LANE), 0)

    @pl.when(step == 0)
    def _():
        att_acc[...] = jnp.zeros_like(att_acc)
        cal_acc[...] = jnp.zeros_like(cal_acc)
        tile_s[...] = jnp.zeros_like(tile_s)

    hot_rows = lax.broadcasted_iota(jnp.int32, (SRC_BLK, SLOT_BLK), 0)
    slot = lax.broadcasted_iota(jnp.int32, (1, SLOT_BLK), 1)
    tile_s[0:5, :] = par_ref[...]
    tile_s[5:6, :] = pre_ref[...]
    for g in range(GRP):
        lanes = slice(g * SLOT_BLK, (g + 1) * SLOT_BLK)
        live = slot < count_ref[step * GRP + g]
        ids = jnp.where(live, src_ref[:, lanes], -1)
        hot = jnp.where(hot_rows == ids, 1.0, 0.0).astype(BF16)
        hot_s[g] = hot
        tile = tile_s[:, lanes]
        prods = jnp.concatenate([tile * tile[p:p + 1, :] for p in range(5)], axis=0)
        stacked = jnp.concatenate(split3(prods), axis=0).astype(BF16)
        sums = lax.dot_general(stacked, hot, NT, preferred_element_type=F32)
        sums_s[:, g, :] = sums[0:40] + sums[40:80] + sums[80:120]
    matrix = [[None] * 5 for _ in range(5)]
    for i in range(5):
        for j in range(i, 5):
            entry = sums_s[i * 8 + j] + (1.0 if i == j else 0.0)
            matrix[i][j] = entry
            matrix[j][i] = entry
    answer = spd_solve(matrix, [sums_s[i * 8 + 5] for i in range(5)])
    for p in range(5):
        upd_s[p] = answer[p]
    upd_s[5] = jnp.zeros((8, LANE), F32)
    upd_s[6] = jnp.zeros((8, LANE), F32)
    upd_s[7] = jnp.zeros((8, LANE), F32)
    for g in range(GRP):
        lanes = slice(g * SLOT_BLK, (g + 1) * SLOT_BLK)
        mine = upd_s[:, g, :]
        upd_ref[:, g * SRC_BLK:(g + 1) * SRC_BLK] = mine[0:5]
        stacked = jnp.concatenate(split3(mine), axis=0).astype(BF16)
        back = jnp.dot(stacked, hot_s[g], preferred_element_type=F32)
        back = back[0:8] + back[8:16] + back[16:24]
        live = slot < count_ref[step * GRP + g]
        fitted = jnp.sum(back * tile_s[:, lanes], axis=0, keepdims=True)
        resid_s[:, lanes] = jnp.where(live, pre_ref[:, lanes] - fitted, 0.0)
        unit_s[:, lanes] = jnp.where(live, unit_ref[:, lanes], -1)

    low8 = row8 < 4
    kk = jnp.bitwise_and(row8, 3)
    c0 = jnp.where(kk == 0, 1.0, jnp.where(kk == 1, 4.0, jnp.where(kk == 2, 1.0, 0.0))) / 6.0
    c1 = jnp.where(kk == 0, -3.0, jnp.where(kk == 2, 3.0, 0.0)) / 6.0
    c2 = jnp.where(kk == 0, 3.0, jnp.where(kk == 1, -6.0, jnp.where(kk == 2, 3.0, 0.0))) / 6.0
    c3 = jnp.where(kk == 0, -1.0, jnp.where(kk == 1, 3.0, jnp.where(kk == 2, -3.0, 1.0))) / 6.0
    half16 = jnp.where(row16 < 8, 0.0, 1.0)
    mod16 = jnp.bitwise_and(row16, 7).astype(F32).astype(BF16)
    iota16 = row16.astype(F32).astype(BF16)
    zero16 = jnp.zeros((16, LANE), BF16)

    def wide16(row):
        return jnp.broadcast_to(row, (16, LANE))

    def build(lane_at, spot):
        at = pl.ds(lane_at, LANE)
        to = pl.ds(spot, LANE)
        resid = resid_s[:, at]
        att4 = att_ref[:, at] * resid
        v8 = jnp.concatenate([att4, att4], axis=0)
        top = rounded(v8)
        v8 = jnp.where(low8, top, v8 - top)
        v16 = jnp.concatenate([v8, v8], axis=0).astype(BF16)
        interval = (rng_ref[:, at] * 256 + knot_ref[:, at]).astype(F32)
        hi = jnp.floor((interval + 0.5) * (1.0 / ATT_BASE))
        lo = interval - hi * ATT_BASE
        hi16 = (wide16(hi) - half16).astype(BF16)
        for t in range(ATT_HI // 2):
            att_a[t * 16:(t + 1) * 16, to] = jnp.where(hi16 == jnp.array(2 * t, BF16), v16, zero16)
        u = jnp.broadcast_to(pos_ref[:, at], (8, LANE))
        w8 = c0 + u * (c1 + u * (c2 + u * c3))
        top = rounded(w8)
        w8 = jnp.where(low8, top, w8 - top)
        los = [wide16(lo + float(k)).astype(BF16) for k in range(4)]
        ws = [wide16(w8[k:k + 1, :]).astype(BF16) for k in range(8)]
        for t in range(8):
            rows = iota16 + jnp.array(16 * t, BF16)
            top_part = zero16
            low_part = zero16
            for k in range(4):
                same = rows == los[k]
                top_part = jnp.where(same, ws[k], top_part)
                low_part = jnp.where(same, ws[4 + k], low_part)
            att_b[t * 16:(t + 1) * 16, to] = top_part
            att_b[128 + t * 16:128 + (t + 1) * 16, to] = low_part
        unit = unit_s[:, at].astype(F32)
        uhi = jnp.floor((unit + 0.5) * (1.0 / CAL_BASE))
        ulo = unit - uhi * CAL_BASE
        same = wide16(uhi).astype(BF16) == mod16
        g8 = [jnp.broadcast_to(cal_ref[p:p + 1, at], (8, LANE)) for p in range(3)]
        r8 = jnp.broadcast_to(resid, (8, LANE))
        terms = [g8[i] * g8[j] for i in range(3) for j in range(i, 3)] + [g8[i] * r8 for i in range(3)]
        for t in range(9):
            top = rounded(terms[t])
            both = jnp.concatenate([top, terms[t] - top], axis=0).astype(BF16)
            cal_a[t * 16:(t + 1) * 16, to] = jnp.where(same, both, zero16)
        ul16 = wide16(ulo).astype(BF16)
        one16 = jnp.ones((16, LANE), BF16)
        for t in range(16):
            rows = iota16 + jnp.array(16 * t, BF16)
            cal_b[t * 16:(t + 1) * 16, to] = jnp.where(rows == ul16, one16, zero16)

    chunk = att_a.shape[1]

    def turn(turn_at, _):
        start = turn_at * chunk
        for j in range(chunk // LANE):
            build(pl.multiple_of(start + j * LANE, LANE), j * LANE)
        att_acc[...] += lax.dot_general(att_a[...], att_b[...], NT, preferred_element_type=F32)
        cal_acc[...] += lax.dot_general(cal_a[...], cal_b[...], NT, preferred_element_type=F32)
        return 0

    lax.fori_loop(0, GRP * SLOT_BLK // chunk, turn, 0)

    @pl.when(step == pl.num_programs(0) - 1)
    def _():
        att_out[...] = jnp.zeros_like(att_out)
        lane = lax.broadcasted_iota(jnp.int32, (4, LANE), 1)
        for h in range(ATT_HI):
            rows = att_acc[h * 8:(h + 1) * 8, :]
            rows = rows[:, :LANE] + rows[:, LANE:]
            piece = rows[0:4] + rows[4:8]
            where, shift = divmod(h * ATT_BASE, LANE)
            turned = pltpu.roll(piece, shift, 1) if shift else piece
            for part in range(2):
                spot = where + part
                if spot >= 64 or (part == 1 and shift == 0):
                    continue
                keep = lane >= shift if part == 0 else lane < shift
                at = slice((spot % 2) * 4, (spot % 2) * 4 + 4)
                att_out[spot // 2, at, :] += jnp.where(keep, turned, 0.0)
        for t in range(9):
            rows = cal_acc[t * 16:(t + 1) * 16, :]
            cal_out[t] = rows[0:8] + rows[8:16]


def obs_call(chunk=640):
    wide = GRP * SLOT_BLK

    def call(block_count, prefit, partials, attitude, position, calib, source, rng, knot, unit):
        blocks = block_count.shape[0]
        steps = blocks // GRP
        row = pl.BlockSpec((1, wide), lambda s, c: (0, s))
        flat = lambda value: value.reshape(1, -1)
        return pl.pallas_call(
            obs_kernel,
            grid_spec=pltpu.PrefetchScalarGridSpec(
                num_scalar_prefetch=1,
                grid=(steps,),
                in_specs=[
                    row,
                    pl.BlockSpec((5, wide), lambda s, c: (0, s)),
                    pl.BlockSpec((4, wide), lambda s, c: (0, s)),
                    row,
                    pl.BlockSpec((3, wide), lambda s, c: (0, s)),
                    row, row, row, row,
                ],
                out_specs=[
                    pl.BlockSpec((5, GRP * SRC_BLK), lambda s, c: (0, s)),
                    pl.BlockSpec((32, 8, LANE), lambda s, c: (0, 0, 0)),
                    pl.BlockSpec((9, 8, 256), lambda s, c: (0, 0, 0)),
                ],
                scratch_shapes=[
                    pltpu.VMEM((8, wide), F32),
                    pltpu.VMEM((GRP, SRC_BLK, SLOT_BLK), BF16),
                    pltpu.VMEM((40, GRP, LANE), F32),
                    pltpu.VMEM((8, GRP, LANE), F32),
                    pltpu.VMEM((1, wide), F32),
                    pltpu.VMEM((1, wide), jnp.int32),
                    pltpu.VMEM((ATT_HI * 8, chunk), BF16),
                    pltpu.VMEM((256, chunk), BF16),
                    pltpu.VMEM((144, chunk), BF16),
                    pltpu.VMEM((256, chunk), BF16),
                    pltpu.VMEM((ATT_HI * 8, 256), F32),
                    pltpu.VMEM((144, 256), F32),
                ],
            ),
            out_shape=[
                jax.ShapeDtypeStruct((5, blocks * SRC_BLK), F32),
                jax.ShapeDtypeStruct((32, 8, LANE), F32),
                jax.ShapeDtypeStruct((9, 8, 256), F32),
            ],
            compiler_params=pltpu.CompilerParams(vmem_limit_bytes=40 * 1024 * 1024),
        )(block_count, flat(prefit), partials, attitude, flat(position), calib, flat(source), flat(rng), flat(knot), flat(unit))

    return call


def join_kernel(recv_ref, inv_ref, decay_ref, send_ref, mul_ref, add_ref):
    total = recv_ref[0]
    for d in range(1, recv_ref.shape[0]):
        total = total + recv_ref[d]
    acc = jnp.zeros((8, 1024), F32)
    for half in range(2):
        for c in range(4):
            spot = half * 4 + c
            col = jnp.broadcast_to(total[spot:spot + 1, :], (LANE, LANE)).T
            first = c * 256 + half * LANE
            for s in range(LANE // 8):
                line = inv_ref[0, first + s * 8:first + s * 8 + 8, :]
                acc = acc + line * jnp.concatenate([col[s * 8:s * 8 + 8, :]] * 8, axis=1)
    flat = jnp.sum(acc, axis=0, keepdims=True)
    solved = jnp.concatenate([flat[:, c * 256:(c + 1) * 256] for c in range(4)], axis=0)
    decay = decay_ref[...]
    mul = decay
    add = jnp.sqrt(1.0 - decay * decay) * solved
    lane = lax.broadcasted_iota(jnp.int32, (4, 256), 1)
    shift = 1
    while shift < 256:
        inside = lane >= shift
        add = add + jnp.where(inside, mul * pltpu.roll(add, shift, 1), 0.0)
        mul = jnp.where(inside, mul * pltpu.roll(mul, shift, 1), mul)
        shift *= 2
    mul_ref[...] = mul
    add_ref[...] = add
    ends = jnp.where(
        lane[:, :LANE] < 64,
        jnp.broadcast_to(mul[:, 255:256], (4, LANE)),
        jnp.broadcast_to(add[:, 255:256], (4, LANE)),
    )
    out = jnp.concatenate([total[8:10], jnp.zeros((2, LANE), F32), ends], axis=0)
    send_ref[...] = jnp.broadcast_to(out[None], send_ref.shape)


def last_kernel(mine_ref, recv_ref, mul_ref, add_ref, att_ref, cal_ref):
    mine = mine_ref[0]
    lane = lax.broadcasted_iota(jnp.int32, (4, LANE), 1)
    state = jnp.zeros((4, LANE), F32)
    for r in range(31):
        ends = recv_ref[r, 4:8, :]
        turned = pltpu.roll(ends, 64, 1)
        longer = jnp.where(lane < 64, ends, turned) * state + jnp.where(lane < 64, turned, ends)
        state = jnp.where(r < mine, longer, state)
    att_ref[...] = add_ref[...] + mul_ref[...] * jnp.concatenate([state, state], axis=1)
    sums = [
        jnp.concatenate([recv_ref[2 * t, 0:2, :], recv_ref[2 * t + 1, 0:2, :]], axis=0)
        for t in range(9)
    ]
    matrix = [[None] * 3 for _ in range(3)]
    slot = 0
    for i in range(3):
        for j in range(i, 3):
            matrix[i][j] = sums[slot] + (1.0 if i == j else 0.0)
            matrix[j][i] = matrix[i][j]
            slot += 1
    answer = spd_solve(matrix, sums[6:9])
    rest = CAL_BASE - LANE
    for p in range(3):
        for par in range(2):
            first = par * CAL_BASE
            cal_ref[p:p + 1, first:first + LANE] = answer[p][2 * par:2 * par + 1, :]
            cal_ref[p:p + 1, first + LANE:first + CAL_BASE] = answer[p][2 * par + 1:2 * par + 2, :rest]


def on_device(
    prefit_resid, source_partials, attitude_partials, spline_position, calib_partials, obs_source,
    block_count, obs_range, obs_knot, obs_unit, given_inverse, knot_decay,
):
    update, att, cal = obs_call(CHUNK)(
        block_count, prefit_resid, source_partials, attitude_partials, spline_position,
        calib_partials, obs_source, obs_range, obs_knot, obs_unit,
    )
    rows = cal.reshape(9, 4, 2, 2, LANE).transpose(0, 2, 1, 3, 4).reshape(18, 4, 2, LANE)
    rows = jnp.pad(rows, ((0, 14), (0, 0), (0, 0), (0, 0)))
    packed = jnp.concatenate([jnp.broadcast_to(att[:, None], (32, 4, 8, LANE)), rows], axis=2)
    recv = lax.all_to_all(packed.reshape(128, 10, LANE), ("wide", "narrow"), 0, 0)
    big = pltpu.CompilerParams(vmem_limit_bytes=40 * 1024 * 1024)
    small = jax.ShapeDtypeStruct((4, 256), F32)
    send, mul, add = pl.pallas_call(
        join_kernel,
        out_shape=[jax.ShapeDtypeStruct((32, 8, LANE), F32), small, small],
        compiler_params=big,
    )(recv, given_inverse, knot_decay)
    again = lax.all_to_all(send, "wide", 0, 0)
    mine = lax.axis_index("wide").reshape(1).astype(jnp.int32)
    att_update, cal_update = pl.pallas_call(
        last_kernel,
        in_specs=[pl.BlockSpec(memory_space=pltpu.SMEM)] + [pl.BlockSpec(memory_space=pltpu.VMEM)] * 3,
        out_shape=[small, jax.ShapeDtypeStruct((3, 504), F32)],
    )(mine, again, mul, add)
    return update, att_update, cal_update


def solution(mesh):
    both = ("wide", "narrow")
    placed = (
        P(both), P(None, both), P(None, both), P(both), P(None, both), P(both),
        P(both), P(both), P(both), P(both), P("wide", None, None), P(None, "wide"),
    )
    return jax.shard_map(
        on_device,
        mesh=mesh,
        in_specs=placed,
        out_specs=(P(None, both), P(None, "wide"), P(None, "narrow")),
        check_vma=False,
    )
```

```python
import jax
import jax.numpy as jnp
from jax import lax
from jax.experimental import pallas as pl
from jax.experimental.pallas import tpu as pltpu
from jax.sharding import PartitionSpec as P

SRC_BLK = 128
SLOT_BLK = 640
CAL = 2016
GRP = 8
CHUNK = 1280
VMEM_OBS = 60 * 1024 * 1024
LANE = 128
ATT_BASE = 125
ATT_HI = 66
CAL_BASE = 252
CAL_HI = 8
F32 = jnp.float32
BF16 = jnp.bfloat16


def rounded(value):
    return value.astype(BF16).astype(F32)


def split3(value):
    top = rounded(value)
    rest = value - top
    mid = rounded(rest)
    return top, mid, rest - mid


def spd_solve(matrix, target):
    order = len(target)
    lower = [[None] * order for _ in range(order)]
    inv = [None] * order
    for col in range(order):
        pivot = matrix[col][col]
        for k in range(col):
            pivot = pivot - lower[col][k] * lower[col][k]
        inv[col] = 1.0 / jnp.sqrt(pivot)
        for row in range(col + 1, order):
            entry = matrix[row][col]
            for k in range(col):
                entry = entry - lower[row][k] * lower[col][k]
            lower[row][col] = entry * inv[col]
    forward = []
    for row in range(order):
        running = target[row]
        for k in range(row):
            running = running - lower[row][k] * forward[k]
        forward.append(running * inv[row])
    answer = [None] * order
    for row in reversed(range(order)):
        running = forward[row]
        for k in range(row + 1, order):
            running = running - lower[k][row] * answer[k]
        answer[row] = running * inv[row]
    return answer


NT = (((1,), (1,)), ((), ()))


def obs_kernel(
    count_ref, pre_ref, par_ref, att_ref, pos_ref, cal_ref, src_ref, rng_ref, knot_ref, unit_ref,
    upd_ref, att_out,
    tile_s, hot_s, sums_s, upd_s, resid_s, unit_s, att_a, att_b, cal_a, cal_b, att_acc, cal_acc, cal_sum,
):
    step = pl.program_id(0)
    row8 = lax.broadcasted_iota(jnp.int32, (8, LANE), 0)
    row16 = lax.broadcasted_iota(jnp.int32, (16, LANE), 0)

    @pl.when(step == 0)
    def _():
        att_acc[...] = jnp.zeros_like(att_acc)
        cal_acc[...] = jnp.zeros_like(cal_acc)
        tile_s[...] = jnp.zeros_like(tile_s)

    hot_rows = lax.broadcasted_iota(jnp.int32, (SRC_BLK, SLOT_BLK), 0)
    slot = lax.broadcasted_iota(jnp.int32, (1, SLOT_BLK), 1)
    tile_s[0:5, :] = par_ref[...]
    tile_s[5:6, :] = pre_ref[...]
    for g in range(GRP):
        lanes = slice(g * SLOT_BLK, (g + 1) * SLOT_BLK)
        live = slot < count_ref[step * GRP + g]
        ids = jnp.where(live, src_ref[:, lanes], -1)
        hot = jnp.where(hot_rows == ids, 1.0, 0.0).astype(BF16)
        hot_s[g] = hot
        tile = tile_s[:, lanes]
        prods = jnp.concatenate([tile * tile[p:p + 1, :] for p in range(5)], axis=0)
        stacked = jnp.concatenate(split3(prods), axis=0).astype(BF16)
        sums = lax.dot_general(stacked, hot, NT, preferred_element_type=F32)
        sums_s[:, g, :] = sums[0:40] + sums[40:80] + sums[80:120]
    matrix = [[None] * 5 for _ in range(5)]
    for i in range(5):
        for j in range(i, 5):
            entry = sums_s[i * 8 + j] + (1.0 if i == j else 0.0)
            matrix[i][j] = entry
            matrix[j][i] = entry
    answer = spd_solve(matrix, [sums_s[i * 8 + 5] for i in range(5)])
    for p in range(5):
        upd_s[p] = answer[p]
    upd_s[5] = jnp.zeros((8, LANE), F32)
    upd_s[6] = jnp.zeros((8, LANE), F32)
    upd_s[7] = jnp.zeros((8, LANE), F32)
    for g in range(GRP):
        lanes = slice(g * SLOT_BLK, (g + 1) * SLOT_BLK)
        mine = upd_s[:, g, :]
        upd_ref[:, g * SRC_BLK:(g + 1) * SRC_BLK] = mine[0:5]
        stacked = jnp.concatenate(split3(mine), axis=0).astype(BF16)
        back = jnp.dot(stacked, hot_s[g], preferred_element_type=F32)
        back = back[0:8] + back[8:16] + back[16:24]
        live = slot < count_ref[step * GRP + g]
        fitted = jnp.sum(back * tile_s[:, lanes], axis=0, keepdims=True)
        resid_s[:, lanes] = jnp.where(live, pre_ref[:, lanes] - fitted, 0.0)
        unit_s[:, lanes] = jnp.where(live, unit_ref[:, lanes], -1)

    low8 = row8 < 4
    kk = jnp.bitwise_and(row8, 3)
    c0 = jnp.where(kk == 0, 1.0, jnp.where(kk == 1, 4.0, jnp.where(kk == 2, 1.0, 0.0))) / 6.0
    c1 = jnp.where(kk == 0, -3.0, jnp.where(kk == 2, 3.0, 0.0)) / 6.0
    c2 = jnp.where(kk == 0, 3.0, jnp.where(kk == 1, -6.0, jnp.where(kk == 2, 3.0, 0.0))) / 6.0
    c3 = jnp.where(kk == 0, -1.0, jnp.where(kk == 1, 3.0, jnp.where(kk == 2, -3.0, 1.0))) / 6.0
    half16 = jnp.where(row16 < 8, 0.0, 1.0)
    mod16 = jnp.bitwise_and(row16, 7).astype(F32).astype(BF16)
    iota16 = row16.astype(F32).astype(BF16)
    zero16 = jnp.zeros((16, LANE), BF16)

    def wide16(row):
        return jnp.broadcast_to(row, (16, LANE))

    def build(lane_at, spot):
        at = pl.ds(lane_at, LANE)
        to = pl.ds(spot, LANE)
        resid = resid_s[:, at]
        att4 = att_ref[:, at] * resid
        v8 = jnp.concatenate([att4, att4], axis=0)
        top = rounded(v8)
        v8 = jnp.where(low8, top, v8 - top)
        v16 = jnp.concatenate([v8, v8], axis=0).astype(BF16)
        interval = (rng_ref[:, at] * 256 + knot_ref[:, at]).astype(F32)
        hi = jnp.floor((interval + 0.5) * (1.0 / ATT_BASE))
        lo = interval - hi * ATT_BASE
        hi16 = (wide16(hi) - half16).astype(BF16)
        for t in range(ATT_HI // 2):
            att_a[t * 16:(t + 1) * 16, to] = jnp.where(hi16 == jnp.array(2 * t, BF16), v16, zero16)
        u = jnp.broadcast_to(pos_ref[:, at], (8, LANE))
        w8 = c0 + u * (c1 + u * (c2 + u * c3))
        top = rounded(w8)
        w8 = jnp.where(low8, top, w8 - top)
        los = [wide16(lo + float(k)).astype(BF16) for k in range(4)]
        ws = [wide16(w8[k:k + 1, :]).astype(BF16) for k in range(8)]
        for t in range(8):
            rows = iota16 + jnp.array(16 * t, BF16)
            top_part = zero16
            low_part = zero16
            for k in range(4):
                same = rows == los[k]
                top_part = jnp.where(same, ws[k], top_part)
                low_part = jnp.where(same, ws[4 + k], low_part)
            att_b[t * 16:(t + 1) * 16, to] = top_part
            att_b[128 + t * 16:128 + (t + 1) * 16, to] = low_part
        unit = unit_s[:, at].astype(F32)
        uhi = jnp.floor((unit + 0.5) * (1.0 / CAL_BASE))
        ulo = unit - uhi * CAL_BASE
        same = wide16(uhi).astype(BF16) == mod16
        g8 = [jnp.broadcast_to(cal_ref[p:p + 1, at], (8, LANE)) for p in range(3)]
        r8 = jnp.broadcast_to(resid, (8, LANE))
        terms = [g8[i] * g8[j] for i in range(3) for j in range(i, 3)] + [g8[i] * r8 for i in range(3)]
        for t in range(9):
            top = rounded(terms[t])
            both = jnp.concatenate([top, terms[t] - top], axis=0).astype(BF16)
            cal_a[t * 16:(t + 1) * 16, to] = jnp.where(same, both, zero16)
        ul16 = wide16(ulo).astype(BF16)
        one16 = jnp.ones((16, LANE), BF16)
        for t in range(16):
            rows = iota16 + jnp.array(16 * t, BF16)
            cal_b[t * 16:(t + 1) * 16, to] = jnp.where(rows == ul16, one16, zero16)

    chunk = att_a.shape[1]

    def turn(turn_at, _):
        start = turn_at * chunk
        for j in range(chunk // LANE):
            build(pl.multiple_of(start + j * LANE, LANE), j * LANE)
        att_acc[...] += lax.dot_general(att_a[...], att_b[...], NT, preferred_element_type=F32)
        cal_acc[...] += lax.dot_general(cal_a[...], cal_b[...], NT, preferred_element_type=F32)
        return 0

    lax.fori_loop(0, GRP * SLOT_BLK // chunk, turn, 0)

    @pl.when(step == pl.num_programs(0) - 1)
    def _():
        att_out[...] = jnp.zeros_like(att_out)
        lane = lax.broadcasted_iota(jnp.int32, (4, LANE), 1)
        for h in range(ATT_HI):
            rows = att_acc[h * 8:(h + 1) * 8, :]
            rows = rows[:, :LANE] + rows[:, LANE:]
            piece = rows[0:4] + rows[4:8]
            where, shift = divmod(h * ATT_BASE, LANE)
            turned = pltpu.roll(piece, shift, 1) if shift else piece
            for part in range(2):
                spot = where + part
                if spot >= 64 or (part == 1 and shift == 0):
                    continue
                keep = lane >= shift if part == 0 else lane < shift
                at = slice((spot % 2) * 4, (spot % 2) * 4 + 4)
                att_out[spot // 2, at, :] += jnp.where(keep, turned, 0.0)
        for t in range(9):
            rows = cal_acc[t * 16:(t + 1) * 16, :]
            rows = rows[0:8] + rows[8:16]
            for half in range(2):
                cal_sum[half] = rows[:, half * LANE:(half + 1) * LANE]
                for par in range(2):
                    spot = 8 + half * 4
                    att_out[2 * t + par, spot:spot + 4, :] = cal_sum[half, pl.ds(par, 4, stride=2), :]


def obs_call(chunk=640):
    wide = GRP * SLOT_BLK

    def call(block_count, prefit, partials, attitude, position, calib, source, rng, knot, unit):
        blocks = block_count.shape[0]
        steps = blocks // GRP
        row = pl.BlockSpec((1, wide), lambda s, c: (0, s))
        flat = lambda value: value.reshape(1, -1)
        return pl.pallas_call(
            obs_kernel,
            grid_spec=pltpu.PrefetchScalarGridSpec(
                num_scalar_prefetch=1,
                grid=(steps,),
                in_specs=[
                    row,
                    pl.BlockSpec((5, wide), lambda s, c: (0, s)),
                    pl.BlockSpec((4, wide), lambda s, c: (0, s)),
                    row,
                    pl.BlockSpec((3, wide), lambda s, c: (0, s)),
                    row, row, row, row,
                ],
                out_specs=[
                    pl.BlockSpec((5, GRP * SRC_BLK), lambda s, c: (0, s)),
                    pl.BlockSpec((32, 16, LANE), lambda s, c: (0, 0, 0)),
                ],
                scratch_shapes=[
                    pltpu.VMEM((8, wide), F32),
                    pltpu.VMEM((GRP, SRC_BLK, SLOT_BLK), BF16),
                    pltpu.VMEM((40, GRP, LANE), F32),
                    pltpu.VMEM((8, GRP, LANE), F32),
                    pltpu.VMEM((1, wide), F32),
                    pltpu.VMEM((1, wide), jnp.int32),
                    pltpu.VMEM((ATT_HI * 8, chunk), BF16),
                    pltpu.VMEM((256, chunk), BF16),
                    pltpu.VMEM((144, chunk), BF16),
                    pltpu.VMEM((256, chunk), BF16),
                    pltpu.VMEM((ATT_HI * 8, 256), F32),
                    pltpu.VMEM((144, 256), F32),
                    pltpu.VMEM((2, 8, LANE), F32),
                ],
            ),
            out_shape=[
                jax.ShapeDtypeStruct((5, blocks * SRC_BLK), F32),
                jax.ShapeDtypeStruct((32, 16, LANE), F32),
            ],
            compiler_params=pltpu.CompilerParams(vmem_limit_bytes=VMEM_OBS),
        )(block_count, flat(prefit), partials, attitude, flat(position), calib, flat(source), flat(rng), flat(knot), flat(unit))

    return call


def join_kernel(group_ref, own_ref, one_ref, two_ref, three_ref, inv_ref, decay_ref, send_ref, mul_ref, add_ref, rows_s):
    total = own_ref[...] + one_ref[...] + two_ref[...] + three_ref[...]
    rows_s[...] = total
    group = group_ref[0]
    acc = jnp.zeros((8, 1024), F32)
    for half in range(2):
        for c in range(4):
            spot = half * 4 + c
            col = jnp.broadcast_to(total[spot:spot + 1, :], (LANE, LANE)).T
            first = c * 256 + half * LANE
            for s in range(LANE // 8):
                line = inv_ref[0, first + s * 8:first + s * 8 + 8, :]
                acc = acc + line * jnp.concatenate([col[s * 8:s * 8 + 8, :]] * 8, axis=1)
    flat = jnp.sum(acc, axis=0, keepdims=True)
    solved = jnp.concatenate([flat[:, c * 256:(c + 1) * 256] for c in range(4)], axis=0)
    decay = decay_ref[...]
    mul = decay
    add = jnp.sqrt(1.0 - decay * decay) * solved
    lane = lax.broadcasted_iota(jnp.int32, (4, 256), 1)
    shift = 1
    while shift < 256:
        inside = lane >= shift
        add = add + jnp.where(inside, mul * pltpu.roll(add, shift, 1), 0.0)
        mul = jnp.where(inside, mul * pltpu.roll(mul, shift, 1), mul)
        shift *= 2
    mul_ref[...] = mul
    add_ref[...] = add
    ends = jnp.where(
        lane[:, :LANE] < 64,
        jnp.broadcast_to(mul[:, 255:256], (4, LANE)),
        jnp.broadcast_to(add[:, 255:256], (4, LANE)),
    )
    out = jnp.concatenate([rows_s[pl.ds(8 + group, 1), :], rows_s[pl.ds(12 + group, 1), :], jnp.zeros((2, LANE), F32), ends], axis=0)
    send_ref[...] = jnp.broadcast_to(out[None], send_ref.shape)


def last_kernel(mine_ref, recv_ref, mul_ref, add_ref, att_ref, cal_ref):
    mine = mine_ref[0]
    lane = lax.broadcasted_iota(jnp.int32, (4, LANE), 1)
    state = jnp.zeros((4, LANE), F32)
    for r in range(31):
        ends = recv_ref[r, 4:8, :]
        turned = pltpu.roll(ends, 64, 1)
        longer = jnp.where(lane < 64, ends, turned) * state + jnp.where(lane < 64, turned, ends)
        state = jnp.where(r < mine, longer, state)
    att_ref[...] = add_ref[...] + mul_ref[...] * jnp.concatenate([state, state], axis=1)
    sums = [
        jnp.concatenate([recv_ref[2 * t, 0:2, :], recv_ref[2 * t + 1, 0:2, :]], axis=0)
        for t in range(9)
    ]
    matrix = [[None] * 3 for _ in range(3)]
    slot = 0
    for i in range(3):
        for j in range(i, 3):
            matrix[i][j] = sums[slot] + (1.0 if i == j else 0.0)
            matrix[j][i] = matrix[i][j]
            slot += 1
    answer = spd_solve(matrix, sums[6:9])
    rest = CAL_BASE - LANE
    for p in range(3):
        for par in range(2):
            first = par * CAL_BASE
            cal_ref[p:p + 1, first:first + LANE] = answer[p][2 * par:2 * par + 1, :]
            cal_ref[p:p + 1, first + LANE:first + CAL_BASE] = answer[p][2 * par + 1:2 * par + 2, :rest]


def on_device(
    prefit_resid, source_partials, attitude_partials, spline_position, calib_partials, obs_source,
    block_count, obs_range, obs_knot, obs_unit, given_inverse, knot_decay,
):
    update, packed = obs_call(CHUNK)(
        block_count, prefit_resid, source_partials, attitude_partials, spline_position,
        calib_partials, obs_source, obs_range, obs_knot, obs_unit,
    )
    own = jnp.sum(lax.all_to_all(packed, "wide", 0, 0), axis=0)
    others = [
        lax.ppermute(own, "narrow", [(i, (i + shift) % 4) for i in range(4)]) for shift in (1, 2, 3)
    ]
    group = lax.axis_index("narrow").reshape(1).astype(jnp.int32)
    scalar = pl.BlockSpec(memory_space=pltpu.SMEM)
    vector = pl.BlockSpec(memory_space=pltpu.VMEM)
    small = jax.ShapeDtypeStruct((4, 256), F32)
    send, mul, add = pl.pallas_call(
        join_kernel,
        in_specs=[scalar] + [vector] * 6,
        out_shape=[jax.ShapeDtypeStruct((32, 8, LANE), F32), small, small],
        scratch_shapes=[pltpu.VMEM((16, LANE), F32)],
        compiler_params=pltpu.CompilerParams(vmem_limit_bytes=16 * 1024 * 1024),
    )(group, own, *others, given_inverse, knot_decay)
    again = lax.all_to_all(send, "wide", 0, 0)
    mine = lax.axis_index("wide").reshape(1).astype(jnp.int32)
    att_update, cal_update = pl.pallas_call(
        last_kernel,
        in_specs=[scalar] + [vector] * 3,
        out_shape=[small, jax.ShapeDtypeStruct((3, 504), F32)],
        compiler_params=pltpu.CompilerParams(vmem_limit_bytes=16 * 1024 * 1024),
    )(mine, again, mul, add)
    return update, att_update, cal_update


def solution(mesh):
    both = ("wide", "narrow")
    placed = (
        P(both), P(None, both), P(None, both), P(both), P(None, both), P(both),
        P(both), P(both), P(both), P(both), P("wide", None, None), P(None, "wide"),
    )
    return jax.shard_map(
        on_device,
        mesh=mesh,
        in_specs=placed,
        out_specs=(P(None, both), P(None, "wide"), P(None, "narrow")),
        check_vma=False,
    )
```

```python
import jax
import jax.numpy as jnp
from jax import lax
from jax.experimental import pallas as pl
from jax.experimental.pallas import tpu as pltpu
from jax.sharding import PartitionSpec as P

SRC_BLK = 128
SLOT_BLK = 640
CAL = 2016
GRP = 8
TURN = 16
VMEM_OBS = 60 * 1024 * 1024
LANE = 128
ATT_BASE = 125
ATT_HI = 68
CAL_BASE = 252
CAL_HI = 8
F32 = jnp.float32
BF16 = jnp.bfloat16


def rounded(value):
    return value.astype(BF16).astype(F32)


def split3(value):
    top = rounded(value)
    rest = value - top
    mid = rounded(rest)
    return top, mid, rest - mid


def spd_solve(matrix, target):
    order = len(target)
    lower = [[None] * order for _ in range(order)]
    inv = [None] * order
    for col in range(order):
        pivot = matrix[col][col]
        for k in range(col):
            pivot = pivot - lower[col][k] * lower[col][k]
        inv[col] = 1.0 / jnp.sqrt(pivot)
        for row in range(col + 1, order):
            entry = matrix[row][col]
            for k in range(col):
                entry = entry - lower[row][k] * lower[col][k]
            lower[row][col] = entry * inv[col]
    forward = []
    for row in range(order):
        running = target[row]
        for k in range(row):
            running = running - lower[row][k] * forward[k]
        forward.append(running * inv[row])
    answer = [None] * order
    for row in reversed(range(order)):
        running = forward[row]
        for k in range(row + 1, order):
            running = running - lower[k][row] * answer[k]
        answer[row] = running * inv[row]
    return answer


NT = (((1,), (1,)), ((), ()))


def obs_kernel(
    count_ref, pre_hbm, par_hbm, att_hbm, pos_hbm, cal_hbm, src_hbm, rng_hbm, knot_hbm, unit_hbm,
    upd_ref, att_out,
    pre_ref, par_ref, att_ref, pos_ref, cal_ref, src_ref, rng_ref, knot_ref, unit_ref,
    tile_s, sums_s, upd_s, back_s,
    att_acc, cal_acc, cal_sum, start_s, live_s, block_s, sems,
):
    pairs = [
        (pre_hbm, pre_ref), (par_hbm, par_ref), (src_hbm, src_ref), (att_hbm, att_ref), (pos_hbm, pos_ref),
        (cal_hbm, cal_ref), (rng_hbm, rng_ref), (knot_hbm, knot_ref), (unit_hbm, unit_ref),
    ]
    copies = [pltpu.make_async_copy(src, dst, sems.at[i]) for i, (src, dst) in enumerate(pairs)]
    for copy in copies:
        copy.start()
    blocks = count_ref.shape[0]
    tiles = SLOT_BLK // LANE
    row8 = lax.broadcasted_iota(jnp.int32, (8, LANE), 0)
    row16 = lax.broadcasted_iota(jnp.int32, (16, LANE), 0)
    lane1 = lax.broadcasted_iota(jnp.int32, (1, LANE), 1)
    att_out[...] = jnp.zeros_like(att_out)

    def listing(block, spot):
        count = count_ref[block]
        for t in range(tiles):
            start_s[spot + t] = block * SLOT_BLK + t * LANE
            live_s[spot + t] = count - t * LANE
            block_s[spot + t] = block
        return spot + lax.shift_right_logical(count + (LANE - 1), 7)

    used = lax.fori_loop(0, blocks, listing, 0)
    for t in range(TURN):
        start_s[used + t] = 0
        live_s[used + t] = 0
        block_s[used + t] = 0
    turns = lax.div(used + (TURN - 1), TURN)

    for copy in copies[:3]:
        copy.wait()
    low8 = row8 < 4
    kk = jnp.bitwise_and(row8, 3)
    c0 = jnp.where(kk == 0, 1.0, jnp.where(kk == 1, 4.0, jnp.where(kk == 2, 1.0, 0.0))) / 6.0
    c1 = jnp.where(kk == 0, -3.0, jnp.where(kk == 2, 3.0, 0.0)) / 6.0
    c2 = jnp.where(kk == 0, 3.0, jnp.where(kk == 1, -6.0, jnp.where(kk == 2, 3.0, 0.0))) / 6.0
    c3 = jnp.where(kk == 0, -1.0, jnp.where(kk == 1, 3.0, jnp.where(kk == 2, -3.0, 1.0))) / 6.0
    quad16 = lax.shift_right_logical(row16, 2).astype(F32)
    mod16 = jnp.bitwise_and(row16, 7).astype(F32).astype(BF16)
    iota16 = row16.astype(F32).astype(BF16)
    zero16 = jnp.zeros((16, LANE), BF16)
    one16 = jnp.ones((16, LANE), BF16)

    def wide16(row):
        return jnp.broadcast_to(row, (16, LANE))

    def beside(left, right):
        return jnp.concatenate([left, right], axis=1)

    def one_hot(row16, count):
        return [jnp.where(iota16 + jnp.array(16 * t, BF16) == row16, one16, zero16) for t in range(count)]

    def source_tile(block, t):
        at = pl.ds(pl.multiple_of(block * SLOT_BLK + t * LANE, LANE), LANE)
        live = lane1 < count_ref[block] - t * LANE
        ids = jnp.where(live, src_ref[:, at], -1).astype(F32)
        par = par_ref[:, at]
        tile_s[0:5, at] = par
        tile_s[5:6, at] = pre_ref[:, at]
        tile_s[6:8, at] = par[0:2]
        tile = tile_s[:, at]
        turned = [tile] + [pltpu.roll(tile, 8 - d, 0) for d in (1, 2, 3)]
        pieces = []
        for d in (0, 2):
            both = jnp.concatenate([tile * turned[d], tile * turned[d + 1]], axis=0)
            pieces.append([part.astype(BF16) for part in split3(both)])
        return one_hot(wide16(ids).astype(BF16), 8), pieces

    def source_sums(accs):
        def group_sums(group, _):
            for pair in range(GRP // 2):
                unit = pair % 2
                block = group * GRP + 2 * pair
                for t in range(tiles):
                    left_hot, left = source_tile(block, t)
                    right_hot, right = source_tile(block + 1, t)
                    rows = [beside(piece, zero16) for piece in left_hot]
                    rows += [beside(zero16, piece) for piece in right_hot]
                    stage = t % 2 if unit == pair else (t + 1) % 2
                    pltpu.matmul_push_rhs(jnp.concatenate(rows, axis=0), stage, unit, transpose=True)
                    for d in range(2):
                        for k in range(3):
                            pltpu.matmul_acc_lhs(
                                accs[pair][d], beside(left[d][k], right[d][k]), stage if d + k == 0 else None
                            )
            for pair in range(GRP // 2):
                for d in range(2):
                    sums = pltpu.matmul_pop(accs[pair][d])
                    for side in range(2):
                        sums_s[group, 16 * d:16 * d + 16, 2 * pair + side, :] = sums[:, side * LANE:(side + 1) * LANE]
            return 0

        lax.fori_loop(0, blocks // GRP, group_sums, 0)

    pl.run_scoped(
        source_sums, [[pltpu.ACC(pair % 2)((16, 256), F32) for _ in range(2)] for pair in range(GRP // 2)]
    )

    matrix = [[None] * 5 for _ in range(5)]
    for i in range(5):
        for j in range(i, 5):
            apart = j - i
            spot = apart * 8 + i if apart < 4 else 20
            entry = sums_s[:, spot] + (1.0 if i == j else 0.0)
            matrix[i][j] = entry
            matrix[j][i] = entry
    answer = spd_solve(matrix, [sums_s[:, spot] for spot in (13, 21, 26, 19, 12)])
    for p in range(5):
        upd_s[p] = answer[p]
    upd_s[5] = jnp.full(upd_s.shape[1:], -1.0, F32)
    upd_s[6] = jnp.zeros(upd_s.shape[1:], F32)
    upd_s[7] = jnp.zeros(upd_s.shape[1:], F32)
    for block in range(blocks):
        mine = upd_s[:, block // GRP, block % GRP, :]
        back_s[block] = mine
        upd_ref[:, block * SRC_BLK:(block + 1) * SRC_BLK] = mine[0:5]
    for copy in copies[3:]:
        copy.wait()

    def tile_rows(entry):
        at = pl.ds(pl.multiple_of(start_s[entry], LANE), LANE)
        live = lane1 < live_s[entry]
        index = jnp.broadcast_to(src_ref[:, at], (8, LANE))
        picked = jnp.take_along_axis(back_s[block_s[entry]], index, axis=1, mode="promise_in_bounds")
        resid = jnp.where(live, -jnp.sum(picked * tile_s[:, at], axis=0, keepdims=True), 0.0)
        att4 = att_ref[:, at] * resid
        v8 = jnp.concatenate([att4, att4], axis=0)
        top8 = rounded(v8)
        rest8 = v8 - top8
        v16 = [jnp.concatenate([part, part], axis=0).astype(BF16) for part in (top8, rest8)]
        interval = (rng_ref[:, at] * 256 + knot_ref[:, at]).astype(F32)
        hi = jnp.floor((interval + 0.5) * (1.0 / ATT_BASE))
        lo = interval - hi * ATT_BASE
        hi16 = (wide16(hi) - quad16).astype(BF16)
        u = jnp.broadcast_to(pos_ref[:, at], (8, LANE))
        w8 = c0 + u * (c1 + u * (c2 + u * c3))
        top = rounded(w8)
        w8 = jnp.where(low8, top, w8 - top)
        los = [wide16(lo + float(k)).astype(BF16) for k in range(4)]
        ws = [wide16(w8[k:k + 1, :]).astype(BF16) for k in range(8)]
        unit = jnp.where(live, unit_ref[:, at], -1).astype(F32)
        uhi = jnp.floor((unit + 0.5) * (1.0 / CAL_BASE))
        ulo = unit - uhi * CAL_BASE
        same = wide16(uhi).astype(BF16) == mod16
        g8 = [jnp.broadcast_to(cal_ref[p:p + 1, at], (8, LANE)) for p in range(3)]
        r8 = jnp.broadcast_to(resid, (8, LANE))
        terms = [g8[i] * g8[j] for i in range(3) for j in range(i, 3)] + [g8[i] * r8 for i in range(3)]
        pieces = []
        for t in range(9):
            top = rounded(terms[t])
            both = jnp.concatenate([top, terms[t] - top], axis=0).astype(BF16)
            pieces.append(jnp.where(same, both, zero16))
        ul16 = wide16(ulo).astype(BF16)
        return v16, hi16, los, ws, pieces, ul16

    def knot_columns(los, ws):
        tops, lows = [], []
        for t in range(8):
            rows = iota16 + jnp.array(16 * t, BF16)
            top_part = zero16
            low_part = zero16
            for k in range(4):
                same = rows == los[k]
                top_part = jnp.where(same, ws[k], top_part)
                low_part = jnp.where(same, ws[4 + k], low_part)
            tops.append(top_part)
            lows.append(low_part)
        return jnp.concatenate(tops + lows, axis=0)

    def matmuls(att_accs, cal_accs):
        def spend(entry, unit):
            left, right = tile_rows(entry), tile_rows(entry + 1)
            pltpu.matmul_push_rhs(
                beside(knot_columns(left[2], left[3]), knot_columns(right[2], right[3])), 0, unit, transpose=True
            )
            for t in range(ATT_HI // 4):
                step = jnp.array(4 * t, BF16)
                same = [side[1] == step for side in (left, right)]
                for k in range(2):
                    rows = beside(jnp.where(same[0], left[0][k], zero16), jnp.where(same[1], right[0][k], zero16))
                    pltpu.matmul_acc_lhs(att_accs[unit][2 * t + k], rows, 0 if t + k == 0 else None)
            pltpu.matmul_push_rhs(
                beside(jnp.concatenate(one_hot(left[5], 16), axis=0), jnp.concatenate(one_hot(right[5], 16), axis=0)), 1, unit, transpose=True
            )
            for t in range(9):
                pltpu.matmul_acc_lhs(cal_accs[unit][t], beside(left[4][t], right[4][t]), 1 if t == 0 else None)

        def turn(turn_at, _):
            for part in range(TURN // 2):
                spend(turn_at * TURN + 2 * part, part % 2)
            return 0

        lax.fori_loop(0, turns, turn, 0)
        for t in range(ATT_HI // 4):
            parts = [pltpu.matmul_pop(att_accs[unit][2 * t + k]) for unit in range(2) for k in range(2)]
            att_acc[t * 16:(t + 1) * 16, :] = (parts[0] + parts[1]) + (parts[2] + parts[3])
        for t in range(9):
            cal_acc[t * 16:(t + 1) * 16, :] = pltpu.matmul_pop(cal_accs[0][t]) + pltpu.matmul_pop(cal_accs[1][t])

    pl.run_scoped(
        matmuls,
        [[pltpu.ACC(unit)((16, 256), F32) for _ in range(ATT_HI // 2)] for unit in range(2)],
        [[pltpu.ACC(unit)((16, 256), F32) for _ in range(9)] for unit in range(2)],
    )

    lane = lax.broadcasted_iota(jnp.int32, (4, LANE), 1)
    for h in range(ATT_HI):
        rows = att_acc[h * 4:(h + 1) * 4, :]
        piece = rows[:, :LANE] + rows[:, LANE:]
        where, shift = divmod(h * ATT_BASE, LANE)
        turned = pltpu.roll(piece, shift, 1) if shift else piece
        for part in range(2):
            spot = where + part
            if spot >= 64 or (part == 1 and shift == 0):
                continue
            keep = lane >= shift if part == 0 else lane < shift
            at = slice((spot % 2) * 4, (spot % 2) * 4 + 4)
            att_out[spot // 2, at, :] += jnp.where(keep, turned, 0.0)
    for t in range(9):
        rows = cal_acc[t * 16:(t + 1) * 16, :]
        rows = rows[0:8] + rows[8:16]
        for half in range(2):
            cal_sum[half] = rows[:, half * LANE:(half + 1) * LANE]
            for par in range(2):
                spot = 8 + half * 4
                att_out[2 * t + par, spot:spot + 4, :] = cal_sum[half, pl.ds(par, 4, stride=2), :]


def obs_call(block_count, prefit, partials, attitude, position, calib, source, rng, knot, unit):
    blocks = block_count.shape[0]
    count = prefit.shape[0]
    flat = lambda value: value.reshape(1, -1)
    row = lambda kind: pltpu.VMEM((1, count), kind)
    listed = pltpu.SMEM((count // LANE + TURN + 8,), jnp.int32)
    return pl.pallas_call(
        obs_kernel,
        in_specs=[pl.BlockSpec(memory_space=pltpu.SMEM)] + [pl.BlockSpec(memory_space=pl.ANY)] * 9,
        out_specs=[pl.BlockSpec(memory_space=pltpu.VMEM)] * 2,
        out_shape=[
            jax.ShapeDtypeStruct((5, blocks * SRC_BLK), F32),
            jax.ShapeDtypeStruct((32, 16, LANE), F32),
        ],
        scratch_shapes=[
            row(F32), pltpu.VMEM((5, count), F32), pltpu.VMEM((4, count), F32), row(F32),
            pltpu.VMEM((3, count), F32), row(jnp.int32), row(jnp.int32), row(jnp.int32), row(jnp.int32),
            pltpu.VMEM((8, count), F32),
            pltpu.VMEM((blocks // GRP, 32, GRP, LANE), F32),
            pltpu.VMEM((8, blocks // GRP, GRP, LANE), F32),
            pltpu.VMEM((blocks, 8, LANE), F32),
            pltpu.VMEM((ATT_HI * 4, 256), F32),
            pltpu.VMEM((144, 256), F32),
            pltpu.VMEM((2, 8, LANE), F32),
            listed, listed, listed,
            pltpu.SemaphoreType.DMA((9,)),
        ],
        compiler_params=pltpu.CompilerParams(vmem_limit_bytes=VMEM_OBS),
    )(block_count, flat(prefit), partials, attitude, flat(position), calib, flat(source), flat(rng), flat(knot), flat(unit))


def join_kernel(group_ref, own_ref, one_ref, two_ref, three_ref, inv_ref, decay_ref, send_ref, mul_ref, add_ref, rows_s):
    total = own_ref[...] + one_ref[...] + two_ref[...] + three_ref[...]
    rows_s[...] = total
    group = group_ref[0]
    acc = jnp.zeros((8, 1024), F32)
    for half in range(2):
        for c in range(4):
            spot = half * 4 + c
            col = jnp.broadcast_to(total[spot:spot + 1, :], (LANE, LANE)).T
            first = c * 256 + half * LANE
            for s in range(LANE // 8):
                line = inv_ref[0, first + s * 8:first + s * 8 + 8, :]
                acc = acc + line * jnp.concatenate([col[s * 8:s * 8 + 8, :]] * 8, axis=1)
    flat = jnp.sum(acc, axis=0, keepdims=True)
    solved = jnp.concatenate([flat[:, c * 256:(c + 1) * 256] for c in range(4)], axis=0)
    decay = decay_ref[...]
    mul = decay
    add = jnp.sqrt(1.0 - decay * decay) * solved
    lane = lax.broadcasted_iota(jnp.int32, (4, 256), 1)
    shift = 1
    while shift < 256:
        inside = lane >= shift
        add = add + jnp.where(inside, mul * pltpu.roll(add, shift, 1), 0.0)
        mul = jnp.where(inside, mul * pltpu.roll(mul, shift, 1), mul)
        shift *= 2
    mul_ref[...] = mul
    add_ref[...] = add
    ends = jnp.where(
        lane[:, :LANE] < 64,
        jnp.broadcast_to(mul[:, 255:256], (4, LANE)),
        jnp.broadcast_to(add[:, 255:256], (4, LANE)),
    )
    out = jnp.concatenate([rows_s[pl.ds(8 + group, 1), :], rows_s[pl.ds(12 + group, 1), :], jnp.zeros((2, LANE), F32), ends], axis=0)
    send_ref[...] = jnp.broadcast_to(out[None], send_ref.shape)


def last_kernel(mine_ref, recv_ref, mul_ref, add_ref, att_ref, cal_ref):
    mine = mine_ref[0]
    lane = lax.broadcasted_iota(jnp.int32, (4, LANE), 1)
    state = jnp.zeros((4, LANE), F32)
    for r in range(31):
        ends = recv_ref[r, 4:8, :]
        turned = pltpu.roll(ends, 64, 1)
        longer = jnp.where(lane < 64, ends, turned) * state + jnp.where(lane < 64, turned, ends)
        state = jnp.where(r < mine, longer, state)
    att_ref[...] = add_ref[...] + mul_ref[...] * jnp.concatenate([state, state], axis=1)
    sums = [
        jnp.concatenate([recv_ref[2 * t, 0:2, :], recv_ref[2 * t + 1, 0:2, :]], axis=0)
        for t in range(9)
    ]
    matrix = [[None] * 3 for _ in range(3)]
    slot = 0
    for i in range(3):
        for j in range(i, 3):
            matrix[i][j] = sums[slot] + (1.0 if i == j else 0.0)
            matrix[j][i] = matrix[i][j]
            slot += 1
    answer = spd_solve(matrix, sums[6:9])
    rest = CAL_BASE - LANE
    for p in range(3):
        for par in range(2):
            first = par * CAL_BASE
            cal_ref[p:p + 1, first:first + LANE] = answer[p][2 * par:2 * par + 1, :]
            cal_ref[p:p + 1, first + LANE:first + CAL_BASE] = answer[p][2 * par + 1:2 * par + 2, :rest]


def on_device(
    prefit_resid, source_partials, attitude_partials, spline_position, calib_partials, obs_source,
    block_count, obs_range, obs_knot, obs_unit, given_inverse, knot_decay,
):
    update, packed = obs_call(
        block_count, prefit_resid, source_partials, attitude_partials, spline_position,
        calib_partials, obs_source, obs_range, obs_knot, obs_unit,
    )
    own = jnp.sum(lax.all_to_all(packed, "wide", 0, 0), axis=0)
    others = [
        lax.ppermute(own, "narrow", [(i, (i + shift) % 4) for i in range(4)]) for shift in (1, 2, 3)
    ]
    group = lax.axis_index("narrow").reshape(1).astype(jnp.int32)
    scalar = pl.BlockSpec(memory_space=pltpu.SMEM)
    vector = pl.BlockSpec(memory_space=pltpu.VMEM)
    small = jax.ShapeDtypeStruct((4, 256), F32)
    send, mul, add = pl.pallas_call(
        join_kernel,
        in_specs=[scalar] + [vector] * 6,
        out_shape=[jax.ShapeDtypeStruct((32, 8, LANE), F32), small, small],
        scratch_shapes=[pltpu.VMEM((16, LANE), F32)],
        compiler_params=pltpu.CompilerParams(vmem_limit_bytes=16 * 1024 * 1024),
    )(group, own, *others, given_inverse, knot_decay)
    again = lax.all_to_all(send, "wide", 0, 0)
    mine = lax.axis_index("wide").reshape(1).astype(jnp.int32)
    att_update, cal_update = pl.pallas_call(
        last_kernel,
        in_specs=[scalar] + [vector] * 3,
        out_shape=[small, jax.ShapeDtypeStruct((3, 504), F32)],
        compiler_params=pltpu.CompilerParams(vmem_limit_bytes=16 * 1024 * 1024),
    )(mine, again, mul, add)
    return update, att_update, cal_update


def solution(mesh):
    both = ("wide", "narrow")
    placed = (
        P(both), P(None, both), P(None, both), P(both), P(None, both), P(both),
        P(both), P(both), P(both), P(both), P("wide", None, None), P(None, "wide"),
    )
    return jax.shard_map(
        on_device,
        mesh=mesh,
        in_specs=placed,
        out_specs=(P(None, both), P(None, "wide"), P(None, "narrow")),
        check_vma=False,
    )
```

```python
import jax
import jax.numpy as jnp
from jax import lax
from jax.experimental import pallas as pl
from jax.experimental.pallas import tpu as pltpu
from jax.sharding import PartitionSpec as P

SRC_BLK = 128
SLOT_BLK = 640
GRP = 8
TURN = 32
REST = 8
SPAN = 4
VMEM_OBS = 60 * 1024 * 1024
LANE = 128
ATT_BASE = 125
ATT_HI = 68
CAL_BASE = 252
F32 = jnp.float32
BF16 = jnp.bfloat16


def rounded(value):
    return value.astype(BF16).astype(F32)


def split3(value):
    top = rounded(value)
    rest = value - top
    mid = rounded(rest)
    return top, mid, rest - mid


def spd_solve(matrix, target):
    order = len(target)
    lower = [[None] * order for _ in range(order)]
    inv = [None] * order
    for col in range(order):
        pivot = matrix[col][col]
        for k in range(col):
            pivot = pivot - lower[col][k] * lower[col][k]
        inv[col] = 1.0 / jnp.sqrt(pivot)
        for row in range(col + 1, order):
            entry = matrix[row][col]
            for k in range(col):
                entry = entry - lower[row][k] * lower[col][k]
            lower[row][col] = entry * inv[col]
    forward = []
    for row in range(order):
        running = target[row]
        for k in range(row):
            running = running - lower[row][k] * forward[k]
        forward.append(running * inv[row])
    answer = [None] * order
    for row in reversed(range(order)):
        running = forward[row]
        for k in range(row + 1, order):
            running = running - lower[k][row] * answer[k]
        answer[row] = running * inv[row]
    return answer


NT = (((1,), (1,)), ((), ()))


def obs_kernel(
    count_ref, pre_hbm, par_hbm, att_hbm, pos_hbm, cal_hbm, src_hbm, rng_hbm, knot_hbm, unit_hbm,
    upd_ref, att_out,
    pre_ref, par_ref, att_ref, pos_ref, cal_ref, src_ref, rng_ref, knot_ref, unit_ref,
    tile_s, sums_s, upd_s, back_s,
    att_acc, cal_acc, cal_sum, start_s, live_s, block_s, sems,
):
    pairs = [
        (pre_hbm, pre_ref), (par_hbm, par_ref), (src_hbm, src_ref), (att_hbm, att_ref), (pos_hbm, pos_ref),
        (cal_hbm, cal_ref), (rng_hbm, rng_ref), (knot_hbm, knot_ref), (unit_hbm, unit_ref),
    ]
    copies = [pltpu.make_async_copy(src, dst, sems.at[i]) for i, (src, dst) in enumerate(pairs)]
    for copy in copies:
        copy.start()
    blocks = count_ref.shape[0]
    tiles = SLOT_BLK // LANE
    row8 = lax.broadcasted_iota(jnp.int32, (8, LANE), 0)
    row16 = lax.broadcasted_iota(jnp.int32, (16, LANE), 0)
    lane1 = lax.broadcasted_iota(jnp.int32, (1, LANE), 1)
    att_out[...] = jnp.zeros_like(att_out)

    def listing(block, spot):
        count = count_ref[block]
        for t in range(tiles):
            start_s[spot + t] = block * SLOT_BLK + t * LANE
            live_s[spot + t] = count - t * LANE
            block_s[spot + t] = block
        return spot + lax.shift_right_logical(count + (LANE - 1), 7)

    used = lax.fori_loop(0, blocks, listing, 0)
    for t in range(REST):
        start_s[used + t] = 0
        live_s[used + t] = 0
        block_s[used + t] = 0
    turns = lax.div(used, TURN)
    rests = lax.div(used - turns * TURN + (REST - 1), REST)

    for copy in copies[:3]:
        copy.wait()
    low8 = row8 < 4
    kk = jnp.bitwise_and(row8, 3)
    c0 = jnp.where(kk == 0, 1.0, jnp.where(kk == 1, 4.0, jnp.where(kk == 2, 1.0, 0.0))) / 6.0
    c1 = jnp.where(kk == 0, -3.0, jnp.where(kk == 2, 3.0, 0.0)) / 6.0
    c2 = jnp.where(kk == 0, 3.0, jnp.where(kk == 1, -6.0, jnp.where(kk == 2, 3.0, 0.0))) / 6.0
    c3 = jnp.where(kk == 0, -1.0, jnp.where(kk == 1, 3.0, jnp.where(kk == 2, -3.0, 1.0))) / 6.0
    quad16 = lax.shift_right_logical(row16, 2).astype(F32)
    mod16 = jnp.bitwise_and(row16, 7).astype(F32).astype(BF16)
    iota16 = row16.astype(F32).astype(BF16)
    zero16 = jnp.zeros((16, LANE), BF16)
    one16 = jnp.ones((16, LANE), BF16)

    def wide16(row):
        return jnp.broadcast_to(row, (16, LANE))

    def beside(left, right):
        return jnp.concatenate([left, right], axis=1)

    def one_hot(row16, count):
        return [jnp.where(iota16 + jnp.array(16 * t, BF16) == row16, one16, zero16) for t in range(count)]

    def source_tile(block, t):
        at = pl.ds(pl.multiple_of(block * SLOT_BLK + t * LANE, LANE), LANE)
        live = lane1 < count_ref[block] - t * LANE
        ids = jnp.where(live, src_ref[:, at], -1).astype(F32)
        par = par_ref[:, at]
        tile_s[0:5, at] = par
        tile_s[5:6, at] = pre_ref[:, at]
        tile_s[6:8, at] = par[0:2]
        tile = tile_s[:, at]
        turned = [tile] + [pltpu.roll(tile, 8 - d, 0) for d in (1, 2, 3)]
        pieces = []
        for d in (0, 2):
            both = jnp.concatenate([tile * turned[d], tile * turned[d + 1]], axis=0)
            pieces.append([part.astype(BF16) for part in split3(both)])
        return one_hot(wide16(ids).astype(BF16), 8), pieces

    def source_sums(accs):
        def spend_pair(group, pair, mine):
            unit = pair % 2
            block = group * GRP + 2 * pair
            for t in range(tiles):
                left_hot, left = source_tile(block, t)
                right_hot, right = source_tile(block + 1, t)
                rows = [beside(piece, zero16) for piece in left_hot]
                rows += [beside(zero16, piece) for piece in right_hot]
                stage = t % 2 if unit == pair else (t + 1) % 2
                pltpu.matmul_push_rhs(jnp.concatenate(rows, axis=0), stage, unit, transpose=True)
                for d in range(2):
                    for k in range(3):
                        pltpu.matmul_acc_lhs(mine[d], beside(left[d][k], right[d][k]), stage if d + k == 0 else None)

        def keep_pair(group, pair, mine):
            for d in range(2):
                sums = pltpu.matmul_pop(mine[d])
                for side in range(2):
                    sums_s[group, 16 * d:16 * d + 16, 2 * pair + side, :] = sums[:, side * LANE:(side + 1) * LANE]

        def group_sums(turn_at, _):
            for part in range(SPAN):
                for pair in range(GRP // 2):
                    spend_pair(turn_at * SPAN + part, pair, accs[part][pair])
            for part in range(SPAN):
                for pair in range(GRP // 2):
                    keep_pair(turn_at * SPAN + part, pair, accs[part][pair])
            return 0

        lax.fori_loop(0, blocks // (GRP * SPAN), group_sums, 0)

    pl.run_scoped(
        source_sums,
        [
            [[pltpu.ACC(pair % 2)((16, 256), F32) for _ in range(2)] for pair in range(GRP // 2)]
            for _ in range(SPAN)
        ],
    )

    matrix = [[None] * 5 for _ in range(5)]
    for i in range(5):
        for j in range(i, 5):
            apart = j - i
            spot = apart * 8 + i if apart < 4 else 20
            entry = sums_s[:, spot] + (1.0 if i == j else 0.0)
            matrix[i][j] = entry
            matrix[j][i] = entry
    answer = spd_solve(matrix, [sums_s[:, spot] for spot in (13, 21, 26, 19, 12)])
    for p in range(5):
        upd_s[p] = answer[p]
    upd_s[5] = jnp.full(upd_s.shape[1:], -1.0, F32)
    upd_s[6] = jnp.zeros(upd_s.shape[1:], F32)
    upd_s[7] = jnp.zeros(upd_s.shape[1:], F32)
    for block in range(blocks):
        mine = upd_s[:, block // GRP, block % GRP, :]
        back_s[block] = mine
        upd_ref[:, block * SRC_BLK:(block + 1) * SRC_BLK] = mine[0:5]
    for copy in copies[3:]:
        copy.wait()

    def tile_rows(entry):
        at = pl.ds(pl.multiple_of(start_s[entry], LANE), LANE)
        live = lane1 < live_s[entry]
        index = jnp.broadcast_to(src_ref[:, at], (8, LANE))
        picked = jnp.take_along_axis(back_s[block_s[entry]], index, axis=1, mode="promise_in_bounds")
        resid = jnp.where(live, -jnp.sum(picked * tile_s[:, at], axis=0, keepdims=True), 0.0)
        att4 = att_ref[:, at] * resid
        v8 = jnp.concatenate([att4, att4], axis=0)
        top8 = rounded(v8)
        rest8 = v8 - top8
        v16 = [jnp.concatenate([part, part], axis=0).astype(BF16) for part in (top8, rest8)]
        interval = (rng_ref[:, at] * 256 + knot_ref[:, at]).astype(F32)
        hi = jnp.floor((interval + 0.5) * (1.0 / ATT_BASE))
        lo = interval - hi * ATT_BASE
        hi16 = (wide16(hi) - quad16).astype(BF16)
        u = jnp.broadcast_to(pos_ref[:, at], (8, LANE))
        w8 = c0 + u * (c1 + u * (c2 + u * c3))
        top = rounded(w8)
        w8 = jnp.where(low8, top, w8 - top)
        los = [wide16(lo + float(k)).astype(BF16) for k in range(4)]
        ws = [wide16(w8[k:k + 1, :]).astype(BF16) for k in range(8)]
        unit = jnp.where(live, unit_ref[:, at], -1).astype(F32)
        uhi = jnp.floor((unit + 0.5) * (1.0 / CAL_BASE))
        ulo = unit - uhi * CAL_BASE
        same = wide16(uhi).astype(BF16) == mod16
        g8 = [jnp.broadcast_to(cal_ref[p:p + 1, at], (8, LANE)) for p in range(3)]
        r8 = jnp.broadcast_to(resid, (8, LANE))
        terms = [g8[i] * g8[j] for i in range(3) for j in range(i, 3)] + [g8[i] * r8 for i in range(3)]
        pieces = []
        for t in range(9):
            top = rounded(terms[t])
            both = jnp.concatenate([top, terms[t] - top], axis=0).astype(BF16)
            pieces.append(jnp.where(same, both, zero16))
        ul16 = wide16(ulo).astype(BF16)
        return v16, hi16, los, ws, pieces, ul16

    def knot_columns(los, ws):
        tops, lows = [], []
        for t in range(8):
            rows = iota16 + jnp.array(16 * t, BF16)
            top_part = zero16
            low_part = zero16
            for k in range(4):
                same = rows == los[k]
                top_part = jnp.where(same, ws[k], top_part)
                low_part = jnp.where(same, ws[4 + k], low_part)
            tops.append(top_part)
            lows.append(low_part)
        return jnp.concatenate(tops + lows, axis=0)

    def matmuls(att_accs, cal_accs):
        def spend(entry, unit):
            left, right = tile_rows(entry), tile_rows(entry + 1)
            pltpu.matmul_push_rhs(
                beside(knot_columns(left[2], left[3]), knot_columns(right[2], right[3])), 0, unit, transpose=True
            )
            for t in range(ATT_HI // 4):
                step = jnp.array(4 * t, BF16)
                same = [side[1] == step for side in (left, right)]
                for k in range(2):
                    rows = beside(jnp.where(same[0], left[0][k], zero16), jnp.where(same[1], right[0][k], zero16))
                    pltpu.matmul_acc_lhs(att_accs[unit][2 * t + k], rows, 0 if t + k == 0 else None)
            pltpu.matmul_push_rhs(
                beside(jnp.concatenate(one_hot(left[5], 16), axis=0), jnp.concatenate(one_hot(right[5], 16), axis=0)), 1, unit, transpose=True
            )
            for t in range(9):
                pltpu.matmul_acc_lhs(cal_accs[unit][t], beside(left[4][t], right[4][t]), 1 if t == 0 else None)

        def turn(turn_at, _):
            for part in range(TURN // 2):
                spend(turn_at * TURN + 2 * part, part % 2)
            return 0

        def rest(rest_at, _):
            for part in range(REST // 2):
                spend(turns * TURN + rest_at * REST + 2 * part, part % 2)
            return 0

        lax.fori_loop(0, turns, turn, 0)
        lax.fori_loop(0, rests, rest, 0)
        for t in range(ATT_HI // 4):
            parts = [pltpu.matmul_pop(att_accs[unit][2 * t + k]) for unit in range(2) for k in range(2)]
            att_acc[t * 16:(t + 1) * 16, :] = (parts[0] + parts[1]) + (parts[2] + parts[3])
        for t in range(9):
            cal_acc[t * 16:(t + 1) * 16, :] = pltpu.matmul_pop(cal_accs[0][t]) + pltpu.matmul_pop(cal_accs[1][t])

    pl.run_scoped(
        matmuls,
        [[pltpu.ACC(unit)((16, 256), F32) for _ in range(ATT_HI // 2)] for unit in range(2)],
        [[pltpu.ACC(unit)((16, 256), F32) for _ in range(9)] for unit in range(2)],
    )

    lane = lax.broadcasted_iota(jnp.int32, (4, LANE), 1)
    for h in range(ATT_HI):
        rows = att_acc[h * 4:(h + 1) * 4, :]
        piece = rows[:, :LANE] + rows[:, LANE:]
        where, shift = divmod(h * ATT_BASE, LANE)
        turned = pltpu.roll(piece, shift, 1) if shift else piece
        for part in range(2):
            spot = where + part
            if spot >= 64 or (part == 1 and shift == 0):
                continue
            keep = lane >= shift if part == 0 else lane < shift
            at = slice((spot % 2) * 4, (spot % 2) * 4 + 4)
            att_out[spot // 2, at, :] += jnp.where(keep, turned, 0.0)
    for t in range(9):
        rows = cal_acc[t * 16:(t + 1) * 16, :]
        rows = rows[0:8] + rows[8:16]
        for half in range(2):
            cal_sum[half] = rows[:, half * LANE:(half + 1) * LANE]
            for par in range(2):
                spot = 8 + half * 4
                att_out[2 * t + par, spot:spot + 4, :] = cal_sum[half, pl.ds(par, 4, stride=2), :]


def obs_call(block_count, prefit, partials, attitude, position, calib, source, rng, knot, unit):
    blocks = block_count.shape[0]
    count = prefit.shape[0]
    flat = lambda value: value.reshape(1, -1)
    row = lambda kind: pltpu.VMEM((1, count), kind)
    listed = pltpu.SMEM((count // LANE + TURN + 8,), jnp.int32)
    return pl.pallas_call(
        obs_kernel,
        in_specs=[pl.BlockSpec(memory_space=pltpu.SMEM)] + [pl.BlockSpec(memory_space=pl.ANY)] * 9,
        out_specs=[pl.BlockSpec(memory_space=pltpu.VMEM)] * 2,
        out_shape=[
            jax.ShapeDtypeStruct((5, blocks * SRC_BLK), F32),
            jax.ShapeDtypeStruct((32, 16, LANE), F32),
        ],
        scratch_shapes=[
            row(F32), pltpu.VMEM((5, count), F32), pltpu.VMEM((4, count), F32), row(F32),
            pltpu.VMEM((3, count), F32), row(jnp.int32), row(jnp.int32), row(jnp.int32), row(jnp.int32),
            pltpu.VMEM((8, count), F32),
            pltpu.VMEM((blocks // GRP, 32, GRP, LANE), F32),
            pltpu.VMEM((8, blocks // GRP, GRP, LANE), F32),
            pltpu.VMEM((blocks, 8, LANE), F32),
            pltpu.VMEM((ATT_HI * 4, 256), F32),
            pltpu.VMEM((144, 256), F32),
            pltpu.VMEM((2, 8, LANE), F32),
            listed, listed, listed,
            pltpu.SemaphoreType.DMA((9,)),
        ],
        compiler_params=pltpu.CompilerParams(vmem_limit_bytes=VMEM_OBS),
    )(block_count, flat(prefit), partials, attitude, flat(position), calib, flat(source), flat(rng), flat(knot), flat(unit))


def join_kernel(group_ref, own_ref, one_ref, two_ref, three_ref, inv_hbm, decay_ref, send_ref, mul_ref, add_ref, rows_s, inv_ref, sems):
    copies = []
    for spot in range(8):
        rows = pl.ds((spot % 4) * 256 + (spot // 4) * LANE, LANE)
        copies.append(pltpu.make_async_copy(inv_hbm.at[0, rows, :], inv_ref.at[rows, :], sems.at[spot]))
        copies[-1].start()
    total = own_ref[...] + one_ref[...] + two_ref[...] + three_ref[...]
    rows_s[...] = total
    group = group_ref[0]
    acc = jnp.zeros((8, 1024), F32)
    for half in range(2):
        for c in range(4):
            spot = half * 4 + c
            col = jnp.broadcast_to(total[spot:spot + 1, :], (LANE, LANE)).T
            first = c * 256 + half * LANE
            copies[spot].wait()
            for s in range(LANE // 8):
                line = inv_ref[first + s * 8:first + s * 8 + 8, :]
                acc = acc + line * jnp.concatenate([col[s * 8:s * 8 + 8, :]] * 8, axis=1)
    flat = jnp.sum(acc, axis=0, keepdims=True)
    solved = jnp.concatenate([flat[:, c * 256:(c + 1) * 256] for c in range(4)], axis=0)
    decay = decay_ref[...]
    mul = decay
    add = jnp.sqrt(1.0 - decay * decay) * solved
    lane = lax.broadcasted_iota(jnp.int32, (4, 256), 1)
    shift = 1
    while shift < 256:
        inside = lane >= shift
        add = add + jnp.where(inside, mul * pltpu.roll(add, shift, 1), 0.0)
        mul = jnp.where(inside, mul * pltpu.roll(mul, shift, 1), mul)
        shift *= 2
    mul_ref[...] = mul
    add_ref[...] = add
    ends = jnp.where(
        lane[:, :LANE] < 64,
        jnp.broadcast_to(mul[:, 255:256], (4, LANE)),
        jnp.broadcast_to(add[:, 255:256], (4, LANE)),
    )
    out = jnp.concatenate([rows_s[pl.ds(8 + group, 1), :], rows_s[pl.ds(12 + group, 1), :], jnp.zeros((2, LANE), F32), ends], axis=0)
    send_ref[...] = jnp.broadcast_to(out[None], send_ref.shape)


def last_kernel(mine_ref, recv_ref, mul_ref, add_ref, att_ref, cal_ref):
    mine = mine_ref[0]
    lane = lax.broadcasted_iota(jnp.int32, (4, LANE), 1)
    state = jnp.zeros((4, LANE), F32)
    for r in range(31):
        ends = recv_ref[r, 4:8, :]
        turned = pltpu.roll(ends, 64, 1)
        longer = jnp.where(lane < 64, ends, turned) * state + jnp.where(lane < 64, turned, ends)
        state = jnp.where(r < mine, longer, state)
    att_ref[...] = add_ref[...] + mul_ref[...] * jnp.concatenate([state, state], axis=1)
    sums = [
        jnp.concatenate([recv_ref[2 * t, 0:2, :], recv_ref[2 * t + 1, 0:2, :]], axis=0)
        for t in range(9)
    ]
    matrix = [[None] * 3 for _ in range(3)]
    slot = 0
    for i in range(3):
        for j in range(i, 3):
            matrix[i][j] = sums[slot] + (1.0 if i == j else 0.0)
            matrix[j][i] = matrix[i][j]
            slot += 1
    answer = spd_solve(matrix, sums[6:9])
    rest = CAL_BASE - LANE
    for p in range(3):
        for par in range(2):
            first = par * CAL_BASE
            cal_ref[p:p + 1, first:first + LANE] = answer[p][2 * par:2 * par + 1, :]
            cal_ref[p:p + 1, first + LANE:first + CAL_BASE] = answer[p][2 * par + 1:2 * par + 2, :rest]


def on_device(
    prefit_resid, source_partials, attitude_partials, spline_position, calib_partials, obs_source,
    block_count, obs_range, obs_knot, obs_unit, given_inverse, knot_decay,
):
    update, packed = obs_call(
        block_count, prefit_resid, source_partials, attitude_partials, spline_position,
        calib_partials, obs_source, obs_range, obs_knot, obs_unit,
    )
    own = jnp.sum(lax.all_to_all(packed, "wide", 0, 0), axis=0)
    others = [
        lax.ppermute(own, "narrow", [(i, (i + shift) % 4) for i in range(4)]) for shift in (1, 2, 3)
    ]
    group = lax.axis_index("narrow").reshape(1).astype(jnp.int32)
    scalar = pl.BlockSpec(memory_space=pltpu.SMEM)
    vector = pl.BlockSpec(memory_space=pltpu.VMEM)
    small = jax.ShapeDtypeStruct((4, 256), F32)
    send, mul, add = pl.pallas_call(
        join_kernel,
        in_specs=[scalar] + [vector] * 4 + [pl.BlockSpec(memory_space=pl.ANY), vector],
        out_shape=[jax.ShapeDtypeStruct((32, 8, LANE), F32), small, small],
        scratch_shapes=[
            pltpu.VMEM((16, LANE), F32),
            pltpu.VMEM(given_inverse.shape[1:], F32),
            pltpu.SemaphoreType.DMA((8,)),
        ],
        compiler_params=pltpu.CompilerParams(vmem_limit_bytes=52 * 1024 * 1024),
    )(group, own, *others, given_inverse, knot_decay)
    again = lax.all_to_all(send, "wide", 0, 0)
    mine = lax.axis_index("wide").reshape(1).astype(jnp.int32)
    att_update, cal_update = pl.pallas_call(
        last_kernel,
        in_specs=[scalar] + [vector] * 3,
        out_shape=[small, jax.ShapeDtypeStruct((3, 504), F32)],
        compiler_params=pltpu.CompilerParams(vmem_limit_bytes=16 * 1024 * 1024),
    )(mine, again, mul, add)
    return update, att_update, cal_update


def solution(mesh):
    both = ("wide", "narrow")
    placed = (
        P(both), P(None, both), P(None, both), P(both), P(None, both), P(both),
        P(both), P(both), P(both), P(both), P("wide", None, None), P(None, "wide"),
    )
    return jax.shard_map(
        on_device,
        mesh=mesh,
        in_specs=placed,
        out_specs=(P(None, both), P(None, "wide"), P(None, "narrow")),
        check_vma=False,
    )
```

```python
import jax
import jax.numpy as jnp
from jax import lax
from jax.experimental import pallas as pl
from jax.experimental.pallas import tpu as pltpu
from jax.sharding import PartitionSpec as P

SRC_BLK = 128
SLOT_BLK = 640
GRP = 8
TURN = 32
REST = 8
SPAN = 4
VMEM_OBS = 16 * 1024 * 1024
LANE = 128
ATT_BASE = 125
ATT_HI = 68
CAL_BASE = 252
F32 = jnp.float32
BF16 = jnp.bfloat16


def rounded(value):
    return value.astype(BF16).astype(F32)


def split3(value):
    top = rounded(value)
    rest = value - top
    mid = rounded(rest)
    return top, mid, rest - mid


def spd_solve(matrix, target):
    order = len(target)
    lower = [[None] * order for _ in range(order)]
    inv = [None] * order
    for col in range(order):
        pivot = matrix[col][col]
        for k in range(col):
            pivot = pivot - lower[col][k] * lower[col][k]
        inv[col] = 1.0 / jnp.sqrt(pivot)
        for row in range(col + 1, order):
            entry = matrix[row][col]
            for k in range(col):
                entry = entry - lower[row][k] * lower[col][k]
            lower[row][col] = entry * inv[col]
    forward = []
    for row in range(order):
        running = target[row]
        for k in range(row):
            running = running - lower[row][k] * forward[k]
        forward.append(running * inv[row])
    answer = [None] * order
    for row in reversed(range(order)):
        running = forward[row]
        for k in range(row + 1, order):
            running = running - lower[k][row] * answer[k]
        answer[row] = running * inv[row]
    return answer


NT = (((1,), (1,)), ((), ()))


def obs_kernel(
    count_ref, pre_hbm, par_hbm, att_hbm, pos_hbm, cal_hbm, src_hbm, rng_hbm, knot_hbm, unit_hbm,
    upd_ref, att_out,
    pre_ref, par_ref, att_ref, pos_ref, cal_ref, src_ref, rng_ref, knot_ref, unit_ref,
    tile_s, sums_s, upd_s, back_s,
    att_acc, cal_acc, cal_sum, start_s, live_s, block_s, sems,
):
    pairs = [
        (pre_hbm, pre_ref), (par_hbm, par_ref), (src_hbm, src_ref), (att_hbm, att_ref), (pos_hbm, pos_ref),
        (cal_hbm, cal_ref), (rng_hbm, rng_ref), (knot_hbm, knot_ref), (unit_hbm, unit_ref),
    ]
    copies = [pltpu.make_async_copy(src, dst, sems.at[i]) for i, (src, dst) in enumerate(pairs)]
    for copy in copies:
        copy.start()
    blocks = count_ref.shape[0]
    tiles = SLOT_BLK // LANE
    row8 = lax.broadcasted_iota(jnp.int32, (8, LANE), 0)
    row16 = lax.broadcasted_iota(jnp.int32, (16, LANE), 0)
    lane1 = lax.broadcasted_iota(jnp.int32, (1, LANE), 1)
    att_out[...] = jnp.zeros_like(att_out)

    def listing(block, spot):
        count = count_ref[block]
        for t in range(tiles):
            start_s[spot + t] = block * SLOT_BLK + t * LANE
            live_s[spot + t] = count - t * LANE
            block_s[spot + t] = block
        return spot + lax.shift_right_logical(count + (LANE - 1), 7)

    used = lax.fori_loop(0, blocks, listing, 0)
    for t in range(REST):
        start_s[used + t] = 0
        live_s[used + t] = 0
        block_s[used + t] = 0
    turns = lax.div(used, TURN)
    rests = lax.div(used - turns * TURN + (REST - 1), REST)

    for copy in copies[:3]:
        copy.wait()
    low8 = row8 < 4
    kk = jnp.bitwise_and(row8, 3)
    c0 = jnp.where(kk == 0, 1.0, jnp.where(kk == 1, 4.0, jnp.where(kk == 2, 1.0, 0.0))) / 6.0
    c1 = jnp.where(kk == 0, -3.0, jnp.where(kk == 2, 3.0, 0.0)) / 6.0
    c2 = jnp.where(kk == 0, 3.0, jnp.where(kk == 1, -6.0, jnp.where(kk == 2, 3.0, 0.0))) / 6.0
    c3 = jnp.where(kk == 0, -1.0, jnp.where(kk == 1, 3.0, jnp.where(kk == 2, -3.0, 1.0))) / 6.0
    quad16 = lax.shift_right_logical(row16, 2).astype(F32)
    mod16 = jnp.bitwise_and(row16, 7).astype(F32).astype(BF16)
    iota16 = row16.astype(F32).astype(BF16)
    zero16 = jnp.zeros((16, LANE), BF16)
    one16 = jnp.ones((16, LANE), BF16)

    def wide16(row):
        return jnp.broadcast_to(row, (16, LANE))

    def beside(left, right):
        return jnp.concatenate([left, right], axis=1)

    def one_hot(row16, count):
        return [jnp.where(iota16 + jnp.array(16 * t, BF16) == row16, one16, zero16) for t in range(count)]

    def source_tile(block, t):
        at = pl.ds(pl.multiple_of(block * SLOT_BLK + t * LANE, LANE), LANE)
        live = lane1 < count_ref[block] - t * LANE
        ids = jnp.where(live, src_ref[:, at], -1).astype(F32)
        par = par_ref[:, at]
        tile_s[0:5, at] = par
        tile_s[5:6, at] = pre_ref[:, at]
        tile_s[6:8, at] = par[0:2]
        tile = tile_s[:, at]
        turned = [tile] + [pltpu.roll(tile, 8 - d, 0) for d in (1, 2, 3)]
        pieces = []
        for d in (0, 2):
            both = jnp.concatenate([tile * turned[d], tile * turned[d + 1]], axis=0)
            pieces.append([part.astype(BF16) for part in split3(both)])
        return one_hot(wide16(ids).astype(BF16), 8), pieces

    def source_sums(accs):
        def spend_pair(group, pair, mine):
            unit = pair % 2
            block = group * GRP + 2 * pair
            for t in range(tiles):
                left_hot, left = source_tile(block, t)
                right_hot, right = source_tile(block + 1, t)
                rows = [beside(piece, zero16) for piece in left_hot]
                rows += [beside(zero16, piece) for piece in right_hot]
                stage = t % 2 if unit == pair else (t + 1) % 2
                pltpu.matmul_push_rhs(jnp.concatenate(rows, axis=0), stage, unit, transpose=True)
                for d in range(2):
                    for k in range(3):
                        pltpu.matmul_acc_lhs(mine[d], beside(left[d][k], right[d][k]), stage if d + k == 0 else None)

        def keep_pair(group, pair, mine):
            for d in range(2):
                sums = pltpu.matmul_pop(mine[d])
                for side in range(2):
                    sums_s[group, 16 * d:16 * d + 16, 2 * pair + side, :] = sums[:, side * LANE:(side + 1) * LANE]

        def group_sums(turn_at, _):
            for part in range(SPAN):
                for pair in range(GRP // 2):
                    spend_pair(turn_at * SPAN + part, pair, accs[part][pair])
            for part in range(SPAN):
                for pair in range(GRP // 2):
                    keep_pair(turn_at * SPAN + part, pair, accs[part][pair])
            return 0

        lax.fori_loop(0, blocks // (GRP * SPAN), group_sums, 0)

    pl.run_scoped(
        source_sums,
        [
            [[pltpu.ACC(pair % 2)((16, 256), F32) for _ in range(2)] for pair in range(GRP // 2)]
            for _ in range(SPAN)
        ],
    )

    matrix = [[None] * 5 for _ in range(5)]
    for i in range(5):
        for j in range(i, 5):
            apart = j - i
            spot = apart * 8 + i if apart < 4 else 20
            entry = sums_s[:, spot] + (1.0 if i == j else 0.0)
            matrix[i][j] = entry
            matrix[j][i] = entry
    answer = spd_solve(matrix, [sums_s[:, spot] for spot in (13, 21, 26, 19, 12)])
    for p in range(5):
        upd_s[p] = answer[p]
    upd_s[5] = jnp.full(upd_s.shape[1:], -1.0, F32)
    upd_s[6] = jnp.zeros(upd_s.shape[1:], F32)
    upd_s[7] = jnp.zeros(upd_s.shape[1:], F32)
    for block in range(blocks):
        mine = upd_s[:, block // GRP, block % GRP, :]
        back_s[block] = mine
        upd_ref[:, block * SRC_BLK:(block + 1) * SRC_BLK] = mine[0:5]
    for copy in copies[3:]:
        copy.wait()

    def tile_rows(entry):
        at = pl.ds(pl.multiple_of(start_s[entry], LANE), LANE)
        live = lane1 < live_s[entry]
        index = jnp.broadcast_to(src_ref[:, at], (8, LANE))
        picked = jnp.take_along_axis(back_s[block_s[entry]], index, axis=1, mode="promise_in_bounds")
        resid = jnp.where(live, -jnp.sum(picked * tile_s[:, at], axis=0, keepdims=True), 0.0)
        att4 = att_ref[:, at] * resid
        v8 = jnp.concatenate([att4, att4], axis=0)
        top8 = rounded(v8)
        rest8 = v8 - top8
        v16 = [jnp.concatenate([part, part], axis=0).astype(BF16) for part in (top8, rest8)]
        interval = (rng_ref[:, at] * 256 + knot_ref[:, at]).astype(F32)
        hi = jnp.floor((interval + 0.5) * (1.0 / ATT_BASE))
        lo = interval - hi * ATT_BASE
        hi16 = (wide16(hi) - quad16).astype(BF16)
        u = jnp.broadcast_to(pos_ref[:, at], (8, LANE))
        w8 = c0 + u * (c1 + u * (c2 + u * c3))
        top = rounded(w8)
        w8 = jnp.where(low8, top, w8 - top)
        los = [wide16(lo + float(k)).astype(BF16) for k in range(4)]
        ws = [wide16(w8[k:k + 1, :]).astype(BF16) for k in range(8)]
        unit = jnp.where(live, unit_ref[:, at], -1).astype(F32)
        uhi = jnp.floor((unit + 0.5) * (1.0 / CAL_BASE))
        ulo = unit - uhi * CAL_BASE
        same = wide16(uhi).astype(BF16) == mod16
        g8 = [jnp.broadcast_to(cal_ref[p:p + 1, at], (8, LANE)) for p in range(3)]
        r8 = jnp.broadcast_to(resid, (8, LANE))
        terms = [g8[i] * g8[j] for i in range(3) for j in range(i, 3)] + [g8[i] * r8 for i in range(3)]
        pieces = []
        for t in range(9):
            top = rounded(terms[t])
            both = jnp.concatenate([top, terms[t] - top], axis=0).astype(BF16)
            pieces.append(jnp.where(same, both, zero16))
        ul16 = wide16(ulo).astype(BF16)
        return v16, hi16, los, ws, pieces, ul16

    def knot_columns(los, ws):
        tops, lows = [], []
        for t in range(8):
            rows = iota16 + jnp.array(16 * t, BF16)
            top_part = zero16
            low_part = zero16
            for k in range(4):
                same = rows == los[k]
                top_part = jnp.where(same, ws[k], top_part)
                low_part = jnp.where(same, ws[4 + k], low_part)
            tops.append(top_part)
            lows.append(low_part)
        return jnp.concatenate(tops + lows, axis=0)

    def matmuls(att_accs, cal_accs):
        def spend(entry, unit):
            left, right = tile_rows(entry), tile_rows(entry + 1)
            pltpu.matmul_push_rhs(
                beside(knot_columns(left[2], left[3]), knot_columns(right[2], right[3])), 0, unit, transpose=True
            )
            for t in range(ATT_HI // 4):
                step = jnp.array(4 * t, BF16)
                same = [side[1] == step for side in (left, right)]
                for k in range(2):
                    rows = beside(jnp.where(same[0], left[0][k], zero16), jnp.where(same[1], right[0][k], zero16))
                    pltpu.matmul_acc_lhs(att_accs[unit][2 * t + k], rows, 0 if t + k == 0 else None)
            pltpu.matmul_push_rhs(
                beside(jnp.concatenate(one_hot(left[5], 16), axis=0), jnp.concatenate(one_hot(right[5], 16), axis=0)), 1, unit, transpose=True
            )
            for t in range(9):
                pltpu.matmul_acc_lhs(cal_accs[unit][t], beside(left[4][t], right[4][t]), 1 if t == 0 else None)

        def turn(turn_at, _):
            for part in range(TURN // 2):
                spend(turn_at * TURN + 2 * part, part % 2)
            return 0

        def rest(rest_at, _):
            for part in range(REST // 2):
                spend(turns * TURN + rest_at * REST + 2 * part, part % 2)
            return 0

        lax.fori_loop(0, turns, turn, 0)
        lax.fori_loop(0, rests, rest, 0)
        for t in range(ATT_HI // 4):
            parts = [pltpu.matmul_pop(att_accs[unit][2 * t + k]) for unit in range(2) for k in range(2)]
            att_acc[t * 16:(t + 1) * 16, :] = (parts[0] + parts[1]) + (parts[2] + parts[3])
        for t in range(9):
            cal_acc[t * 16:(t + 1) * 16, :] = pltpu.matmul_pop(cal_accs[0][t]) + pltpu.matmul_pop(cal_accs[1][t])

    pl.run_scoped(
        matmuls,
        [[pltpu.ACC(unit)((16, 256), F32) for _ in range(ATT_HI // 2)] for unit in range(2)],
        [[pltpu.ACC(unit)((16, 256), F32) for _ in range(9)] for unit in range(2)],
    )

    lane = lax.broadcasted_iota(jnp.int32, (4, LANE), 1)
    for h in range(ATT_HI):
        rows = att_acc[h * 4:(h + 1) * 4, :]
        piece = rows[:, :LANE] + rows[:, LANE:]
        where, shift = divmod(h * ATT_BASE, LANE)
        turned = pltpu.roll(piece, shift, 1) if shift else piece
        for part in range(2):
            spot = where + part
            if spot >= 64 or (part == 1 and shift == 0):
                continue
            keep = lane >= shift if part == 0 else lane < shift
            at = slice((spot % 2) * 4, (spot % 2) * 4 + 4)
            att_out[spot // 2, at, :] += jnp.where(keep, turned, 0.0)
    for t in range(9):
        rows = cal_acc[t * 16:(t + 1) * 16, :]
        rows = rows[0:8] + rows[8:16]
        for half in range(2):
            cal_sum[half] = rows[:, half * LANE:(half + 1) * LANE]
            for par in range(2):
                spot = 8 + half * 4
                att_out[2 * t + par, spot:spot + 4, :] = cal_sum[half, pl.ds(par, 4, stride=2), :]


def obs_call(block_count, prefit, partials, attitude, position, calib, source, rng, knot, unit):
    blocks = block_count.shape[0]
    count = prefit.shape[0]
    pin = lambda value: pltpu.with_memory_space_constraint(value, pltpu.HBM)
    flat = lambda value: pin(value.reshape(1, -1))
    row = lambda kind: pltpu.VMEM((1, count), kind)
    listed = pltpu.SMEM((count // LANE + TURN + 8,), jnp.int32)
    return pl.pallas_call(
        obs_kernel,
        in_specs=[pl.BlockSpec(memory_space=pltpu.SMEM)] + [pl.BlockSpec(memory_space=pltpu.HBM)] * 9,
        out_specs=[pl.BlockSpec(memory_space=pltpu.VMEM)] * 2,
        out_shape=[
            jax.ShapeDtypeStruct((5, blocks * SRC_BLK), F32),
            jax.ShapeDtypeStruct((32, 16, LANE), F32),
        ],
        scratch_shapes=[
            row(F32), pltpu.VMEM((5, count), F32), pltpu.VMEM((4, count), F32), row(F32),
            pltpu.VMEM((3, count), F32), row(jnp.int32), row(jnp.int32), row(jnp.int32), row(jnp.int32),
            pltpu.VMEM((8, count), F32),
            pltpu.VMEM((blocks // GRP, 32, GRP, LANE), F32),
            pltpu.VMEM((8, blocks // GRP, GRP, LANE), F32),
            pltpu.VMEM((blocks, 8, LANE), F32),
            pltpu.VMEM((ATT_HI * 4, 256), F32),
            pltpu.VMEM((144, 256), F32),
            pltpu.VMEM((2, 8, LANE), F32),
            listed, listed, listed,
            pltpu.SemaphoreType.DMA((9,)),
        ],
        compiler_params=pltpu.CompilerParams(vmem_limit_bytes=VMEM_OBS),
    )(pin(block_count), flat(prefit), pin(partials), pin(attitude), flat(position), pin(calib), flat(source), flat(rng), flat(knot), flat(unit))


def join_kernel(group_ref, own_ref, one_ref, two_ref, three_ref, inv_hbm, decay_ref, send_ref, mul_ref, add_ref, rows_s, inv_ref, sems):
    copies = []
    for spot in range(8):
        rows = pl.ds((spot % 4) * 256 + (spot // 4) * LANE, LANE)
        copies.append(pltpu.make_async_copy(inv_hbm.at[0, rows, :], inv_ref.at[rows, :], sems.at[spot]))
        copies[-1].start()
    total = own_ref[...] + one_ref[...] + two_ref[...] + three_ref[...]
    rows_s[...] = total
    group = group_ref[0]
    acc = jnp.zeros((8, 1024), F32)
    for half in range(2):
        for c in range(4):
            spot = half * 4 + c
            col = jnp.broadcast_to(total[spot:spot + 1, :], (LANE, LANE)).T
            first = c * 256 + half * LANE
            copies[spot].wait()
            for s in range(LANE // 8):
                line = inv_ref[first + s * 8:first + s * 8 + 8, :]
                acc = acc + line * jnp.concatenate([col[s * 8:s * 8 + 8, :]] * 8, axis=1)
    flat = jnp.sum(acc, axis=0, keepdims=True)
    solved = jnp.concatenate([flat[:, c * 256:(c + 1) * 256] for c in range(4)], axis=0)
    decay = decay_ref[...]
    mul = decay
    add = jnp.sqrt(1.0 - decay * decay) * solved
    lane = lax.broadcasted_iota(jnp.int32, (4, 256), 1)
    shift = 1
    while shift < 256:
        inside = lane >= shift
        add = add + jnp.where(inside, mul * pltpu.roll(add, shift, 1), 0.0)
        mul = jnp.where(inside, mul * pltpu.roll(mul, shift, 1), mul)
        shift *= 2
    mul_ref[...] = mul
    add_ref[...] = add
    ends = jnp.where(
        lane[:, :LANE] < 64,
        jnp.broadcast_to(mul[:, 255:256], (4, LANE)),
        jnp.broadcast_to(add[:, 255:256], (4, LANE)),
    )
    out = jnp.concatenate([rows_s[pl.ds(8 + group, 1), :], rows_s[pl.ds(12 + group, 1), :], jnp.zeros((2, LANE), F32), ends], axis=0)
    send_ref[...] = jnp.broadcast_to(out[None], send_ref.shape)


def last_kernel(mine_ref, recv_ref, mul_ref, add_ref, att_ref, cal_ref):
    mine = mine_ref[0]
    lane = lax.broadcasted_iota(jnp.int32, (4, LANE), 1)
    state = jnp.zeros((4, LANE), F32)
    for r in range(31):
        ends = recv_ref[r, 4:8, :]
        turned = pltpu.roll(ends, 64, 1)
        longer = jnp.where(lane < 64, ends, turned) * state + jnp.where(lane < 64, turned, ends)
        state = jnp.where(r < mine, longer, state)
    att_ref[...] = add_ref[...] + mul_ref[...] * jnp.concatenate([state, state], axis=1)
    sums = [
        jnp.concatenate([recv_ref[2 * t, 0:2, :], recv_ref[2 * t + 1, 0:2, :]], axis=0)
        for t in range(9)
    ]
    matrix = [[None] * 3 for _ in range(3)]
    slot = 0
    for i in range(3):
        for j in range(i, 3):
            matrix[i][j] = sums[slot] + (1.0 if i == j else 0.0)
            matrix[j][i] = matrix[i][j]
            slot += 1
    answer = spd_solve(matrix, sums[6:9])
    rest = CAL_BASE - LANE
    for p in range(3):
        for par in range(2):
            first = par * CAL_BASE
            cal_ref[p:p + 1, first:first + LANE] = answer[p][2 * par:2 * par + 1, :]
            cal_ref[p:p + 1, first + LANE:first + CAL_BASE] = answer[p][2 * par + 1:2 * par + 2, :rest]


def on_device(
    prefit_resid, source_partials, attitude_partials, spline_position, calib_partials, obs_source,
    block_count, obs_range, obs_knot, obs_unit, given_inverse, knot_decay,
):
    update, packed = obs_call(
        block_count, prefit_resid, source_partials, attitude_partials, spline_position,
        calib_partials, obs_source, obs_range, obs_knot, obs_unit,
    )
    own = jnp.sum(lax.all_to_all(packed, "wide", 0, 0), axis=0)
    others = [
        lax.ppermute(own, "narrow", [(i, (i + shift) % 4) for i in range(4)]) for shift in (1, 2, 3)
    ]
    group = lax.axis_index("narrow").reshape(1).astype(jnp.int32)
    scalar = pl.BlockSpec(memory_space=pltpu.SMEM)
    vector = pl.BlockSpec(memory_space=pltpu.VMEM)
    small = jax.ShapeDtypeStruct((4, 256), F32)
    send, mul, add = pl.pallas_call(
        join_kernel,
        in_specs=[scalar] + [vector] * 4 + [pl.BlockSpec(memory_space=pltpu.HBM), vector],
        out_shape=[jax.ShapeDtypeStruct((32, 8, LANE), F32), small, small],
        scratch_shapes=[
            pltpu.VMEM((16, LANE), F32),
            pltpu.VMEM(given_inverse.shape[1:], F32),
            pltpu.SemaphoreType.DMA((8,)),
        ],
        compiler_params=pltpu.CompilerParams(vmem_limit_bytes=16 * 1024 * 1024),
    )(group, own, *others, pltpu.with_memory_space_constraint(given_inverse, pltpu.HBM), knot_decay)
    again = lax.all_to_all(send, "wide", 0, 0)
    mine = lax.axis_index("wide").reshape(1).astype(jnp.int32)
    att_update, cal_update = pl.pallas_call(
        last_kernel,
        in_specs=[scalar] + [vector] * 3,
        out_shape=[small, jax.ShapeDtypeStruct((3, 504), F32)],
        compiler_params=pltpu.CompilerParams(vmem_limit_bytes=16 * 1024 * 1024),
    )(mine, again, mul, add)
    return update, att_update, cal_update


def solution(mesh):
    both = ("wide", "narrow")
    placed = (
        P(both), P(None, both), P(None, both), P(both), P(None, both), P(both),
        P(both), P(both), P(both), P(both), P("wide", None, None), P(None, "wide"),
    )
    return jax.shard_map(
        on_device,
        mesh=mesh,
        in_specs=placed,
        out_specs=(P(None, both), P(None, "wide"), P(None, "narrow")),
        check_vma=False,
    )
```

```python
import jax
import jax.numpy as jnp
from jax import lax
from jax.experimental import pallas as pl
from jax.experimental.pallas import tpu as pltpu
from jax.sharding import PartitionSpec as P

SRC_BLK = 128
SLOT_BLK = 640
GRP = 8
TURN = 32
REST = 8
SPAN = 4
VMEM_OBS = 16 * 1024 * 1024
LANE = 128
ATT_BASE = 125
ATT_HI = 68
CAL_BASE = 252
F32 = jnp.float32
BF16 = jnp.bfloat16


def rounded(value):
    return value.astype(BF16).astype(F32)


def split3(value):
    top = rounded(value)
    rest = value - top
    mid = rounded(rest)
    return top, mid, rest - mid


def spd_solve(matrix, target):
    order = len(target)
    lower = [[None] * order for _ in range(order)]
    inv = [None] * order
    for col in range(order):
        pivot = matrix[col][col]
        for k in range(col):
            pivot = pivot - lower[col][k] * lower[col][k]
        inv[col] = 1.0 / jnp.sqrt(pivot)
        for row in range(col + 1, order):
            entry = matrix[row][col]
            for k in range(col):
                entry = entry - lower[row][k] * lower[col][k]
            lower[row][col] = entry * inv[col]
    forward = []
    for row in range(order):
        running = target[row]
        for k in range(row):
            running = running - lower[row][k] * forward[k]
        forward.append(running * inv[row])
    answer = [None] * order
    for row in reversed(range(order)):
        running = forward[row]
        for k in range(row + 1, order):
            running = running - lower[k][row] * answer[k]
        answer[row] = running * inv[row]
    return answer


NT = (((1,), (1,)), ((), ()))


def obs_kernel(
    count_ref, pre_hbm, par_hbm, att_hbm, pos_hbm, cal_hbm, src_hbm, rng_hbm, knot_hbm, unit_hbm,
    upd_ref, att_out,
    pre_ref, par_ref, att_ref, pos_ref, cal_ref, src_ref, rng_ref, knot_ref, unit_ref,
    tile_s, sums_s, upd_s, back_s,
    att_acc, cal_acc, cal_sum, start_s, live_s, block_s, sems,
):
    pairs = [
        (pre_hbm, pre_ref), (par_hbm, par_ref), (src_hbm, src_ref), (att_hbm, att_ref), (pos_hbm, pos_ref),
        (cal_hbm, cal_ref), (rng_hbm, rng_ref), (knot_hbm, knot_ref), (unit_hbm, unit_ref),
    ]
    copies = [pltpu.make_async_copy(src, dst, sems.at[i]) for i, (src, dst) in enumerate(pairs)]
    for copy in copies:
        copy.start()
    blocks = count_ref.shape[0]
    tiles = SLOT_BLK // LANE
    row8 = lax.broadcasted_iota(jnp.int32, (8, LANE), 0)
    row16 = lax.broadcasted_iota(jnp.int32, (16, LANE), 0)
    lane1 = lax.broadcasted_iota(jnp.int32, (1, LANE), 1)
    att_out[...] = jnp.zeros_like(att_out)

    def listing(block, spot):
        count = count_ref[block]
        for t in range(tiles):
            start_s[spot + t] = block * SLOT_BLK + t * LANE
            live_s[spot + t] = count - t * LANE
            block_s[spot + t] = block
        return spot + lax.shift_right_logical(count + (LANE - 1), 7)

    used = lax.fori_loop(0, blocks, listing, 0)
    for t in range(REST):
        start_s[used + t] = 0
        live_s[used + t] = 0
        block_s[used + t] = 0
    turns = lax.div(used, TURN)
    rests = lax.div(used - turns * TURN + (REST - 1), REST)

    for copy in copies[:3]:
        copy.wait()
    low8 = row8 < 4
    kk = jnp.bitwise_and(row8, 3)
    c0 = jnp.where(kk == 0, 1.0, jnp.where(kk == 1, 4.0, jnp.where(kk == 2, 1.0, 0.0))) / 6.0
    c1 = jnp.where(kk == 0, -3.0, jnp.where(kk == 2, 3.0, 0.0)) / 6.0
    c2 = jnp.where(kk == 0, 3.0, jnp.where(kk == 1, -6.0, jnp.where(kk == 2, 3.0, 0.0))) / 6.0
    c3 = jnp.where(kk == 0, -1.0, jnp.where(kk == 1, 3.0, jnp.where(kk == 2, -3.0, 1.0))) / 6.0
    quad16 = lax.shift_right_logical(row16, 2).astype(F32)
    mod16 = jnp.bitwise_and(row16, 7).astype(F32).astype(BF16)
    iota16 = row16.astype(F32).astype(BF16)
    zero16 = jnp.zeros((16, LANE), BF16)
    one16 = jnp.ones((16, LANE), BF16)

    def wide16(row):
        return jnp.broadcast_to(row, (16, LANE))

    def beside(left, right):
        return jnp.concatenate([left, right], axis=1)

    def one_hot(row16, count):
        return [jnp.where(iota16 + jnp.array(16 * t, BF16) == row16, one16, zero16) for t in range(count)]

    def source_tile(block, t):
        at = pl.ds(pl.multiple_of(block * SLOT_BLK + t * LANE, LANE), LANE)
        live = lane1 < count_ref[block] - t * LANE
        ids = jnp.where(live, src_ref[:, at], -1).astype(F32)
        par = par_ref[:, at]
        tile_s[0:5, at] = par
        tile_s[5:6, at] = pre_ref[:, at]
        tile_s[6:8, at] = par[0:2]
        tile = tile_s[:, at]
        turned = [tile] + [pltpu.roll(tile, 8 - d, 0) for d in (1, 2, 3)]
        pieces = []
        for d in (0, 2):
            both = jnp.concatenate([tile * turned[d], tile * turned[d + 1]], axis=0)
            pieces.append([part.astype(BF16) for part in split3(both)])
        return one_hot(wide16(ids).astype(BF16), 8), pieces

    def source_sums(accs):
        def spend_pair(group, pair, mine):
            unit = pair % 2
            block = group * GRP + 2 * pair
            for t in range(tiles):
                left_hot, left = source_tile(block, t)
                right_hot, right = source_tile(block + 1, t)
                rows = [beside(piece, zero16) for piece in left_hot]
                rows += [beside(zero16, piece) for piece in right_hot]
                stage = t % 2 if unit == pair else (t + 1) % 2
                pltpu.matmul_push_rhs(jnp.concatenate(rows, axis=0), stage, unit, transpose=True)
                for d in range(2):
                    for k in range(3):
                        pltpu.matmul_acc_lhs(mine[d], beside(left[d][k], right[d][k]), stage if d + k == 0 else None)

        def keep_pair(group, pair, mine):
            for d in range(2):
                sums = pltpu.matmul_pop(mine[d])
                for side in range(2):
                    sums_s[group, 16 * d:16 * d + 16, 2 * pair + side, :] = sums[:, side * LANE:(side + 1) * LANE]

        def group_sums(turn_at, _):
            for part in range(SPAN):
                for pair in range(GRP // 2):
                    spend_pair(turn_at * SPAN + part, pair, accs[part][pair])
            for part in range(SPAN):
                for pair in range(GRP // 2):
                    keep_pair(turn_at * SPAN + part, pair, accs[part][pair])
            return 0

        lax.fori_loop(0, blocks // (GRP * SPAN), group_sums, 0)

    pl.run_scoped(
        source_sums,
        [
            [[pltpu.ACC(pair % 2)((16, 256), F32) for _ in range(2)] for pair in range(GRP // 2)]
            for _ in range(SPAN)
        ],
    )

    matrix = [[None] * 5 for _ in range(5)]
    for i in range(5):
        for j in range(i, 5):
            apart = j - i
            spot = apart * 8 + i if apart < 4 else 20
            entry = sums_s[:, spot] + (1.0 if i == j else 0.0)
            matrix[i][j] = entry
            matrix[j][i] = entry
    answer = spd_solve(matrix, [sums_s[:, spot] for spot in (13, 21, 26, 19, 12)])
    for p in range(5):
        upd_s[p] = answer[p]
    upd_s[5] = jnp.full(upd_s.shape[1:], -1.0, F32)
    upd_s[6] = jnp.zeros(upd_s.shape[1:], F32)
    upd_s[7] = jnp.zeros(upd_s.shape[1:], F32)
    for block in range(blocks):
        mine = upd_s[:, block // GRP, block % GRP, :]
        back_s[block] = mine
        upd_ref[:, block * SRC_BLK:(block + 1) * SRC_BLK] = mine[0:5]
    for copy in copies[3:]:
        copy.wait()

    def tile_rows(entry):
        at = pl.ds(pl.multiple_of(start_s[entry], LANE), LANE)
        live = lane1 < live_s[entry]
        index = jnp.broadcast_to(src_ref[:, at], (8, LANE))
        picked = jnp.take_along_axis(back_s[block_s[entry]], index, axis=1, mode="promise_in_bounds")
        resid = jnp.where(live, -jnp.sum(picked * tile_s[:, at], axis=0, keepdims=True), 0.0)
        att4 = att_ref[:, at] * resid
        v8 = jnp.concatenate([att4, att4], axis=0)
        top8 = rounded(v8)
        rest8 = v8 - top8
        v16 = [jnp.concatenate([part, part], axis=0).astype(BF16) for part in (top8, rest8)]
        interval = (rng_ref[:, at] * 256 + knot_ref[:, at]).astype(F32)
        hi = jnp.floor((interval + 0.5) * (1.0 / ATT_BASE))
        lo = interval - hi * ATT_BASE
        hi16 = (wide16(hi) - quad16).astype(BF16)
        u = jnp.broadcast_to(pos_ref[:, at], (8, LANE))
        w8 = c0 + u * (c1 + u * (c2 + u * c3))
        top = rounded(w8)
        w8 = jnp.where(low8, top, w8 - top)
        los = [wide16(lo + float(k)).astype(BF16) for k in range(4)]
        ws = [wide16(w8[k:k + 1, :]).astype(BF16) for k in range(8)]
        unit = jnp.where(live, unit_ref[:, at], -1).astype(F32)
        uhi = jnp.floor((unit + 0.5) * (1.0 / CAL_BASE))
        ulo = unit - uhi * CAL_BASE
        same = wide16(uhi).astype(BF16) == mod16
        g8 = [jnp.broadcast_to(cal_ref[p:p + 1, at], (8, LANE)) for p in range(3)]
        r8 = jnp.broadcast_to(resid, (8, LANE))
        terms = [g8[i] * g8[j] for i in range(3) for j in range(i, 3)] + [g8[i] * r8 for i in range(3)]
        pieces = []
        for t in range(9):
            top = rounded(terms[t])
            both = jnp.concatenate([top, terms[t] - top], axis=0).astype(BF16)
            pieces.append(jnp.where(same, both, zero16))
        ul16 = wide16(ulo).astype(BF16)
        return v16, hi16, los, ws, pieces, ul16

    def knot_columns(los, ws):
        tops, lows = [], []
        for t in range(8):
            rows = iota16 + jnp.array(16 * t, BF16)
            top_part = zero16
            low_part = zero16
            for k in range(4):
                same = rows == los[k]
                top_part = jnp.where(same, ws[k], top_part)
                low_part = jnp.where(same, ws[4 + k], low_part)
            tops.append(top_part)
            lows.append(low_part)
        return jnp.concatenate(tops + lows, axis=0)

    def matmuls(att_accs, cal_accs):
        def spend(entry, unit):
            left, right = tile_rows(entry), tile_rows(entry + 1)
            pltpu.matmul_push_rhs(
                beside(knot_columns(left[2], left[3]), knot_columns(right[2], right[3])), 0, unit, transpose=True
            )
            for t in range(ATT_HI // 4):
                step = jnp.array(4 * t, BF16)
                same = [side[1] == step for side in (left, right)]
                for k in range(2):
                    rows = beside(jnp.where(same[0], left[0][k], zero16), jnp.where(same[1], right[0][k], zero16))
                    pltpu.matmul_acc_lhs(att_accs[unit][2 * t + k], rows, 0 if t + k == 0 else None)
            pltpu.matmul_push_rhs(
                beside(jnp.concatenate(one_hot(left[5], 16), axis=0), jnp.concatenate(one_hot(right[5], 16), axis=0)), 1, unit, transpose=True
            )
            for t in range(9):
                pltpu.matmul_acc_lhs(cal_accs[unit][t], beside(left[4][t], right[4][t]), 1 if t == 0 else None)

        def turn(turn_at, _):
            for part in range(TURN // 2):
                spend(turn_at * TURN + 2 * part, part % 2)
            return 0

        def rest(rest_at, _):
            for part in range(REST // 2):
                spend(turns * TURN + rest_at * REST + 2 * part, part % 2)
            return 0

        lax.fori_loop(0, turns, turn, 0)
        lax.fori_loop(0, rests, rest, 0)
        for t in range(ATT_HI // 4):
            parts = [pltpu.matmul_pop(att_accs[unit][2 * t + k]) for unit in range(2) for k in range(2)]
            att_acc[t * 16:(t + 1) * 16, :] = (parts[0] + parts[1]) + (parts[2] + parts[3])
        for t in range(9):
            cal_acc[t * 16:(t + 1) * 16, :] = pltpu.matmul_pop(cal_accs[0][t]) + pltpu.matmul_pop(cal_accs[1][t])

    pl.run_scoped(
        matmuls,
        [[pltpu.ACC(unit)((16, 256), F32) for _ in range(ATT_HI // 2)] for unit in range(2)],
        [[pltpu.ACC(unit)((16, 256), F32) for _ in range(9)] for unit in range(2)],
    )

    lane = lax.broadcasted_iota(jnp.int32, (4, LANE), 1)
    for h in range(ATT_HI):
        rows = att_acc[h * 4:(h + 1) * 4, :]
        piece = rows[:, :LANE] + rows[:, LANE:]
        where, shift = divmod(h * ATT_BASE, LANE)
        turned = pltpu.roll(piece, shift, 1) if shift else piece
        for part in range(2):
            spot = where + part
            if spot >= 64 or (part == 1 and shift == 0):
                continue
            keep = lane >= shift if part == 0 else lane < shift
            at = slice((spot % 2) * 4, (spot % 2) * 4 + 4)
            att_out[spot // 2, at, :] += jnp.where(keep, turned, 0.0)
    for t in range(9):
        rows = cal_acc[t * 16:(t + 1) * 16, :]
        rows = rows[0:8] + rows[8:16]
        for half in range(2):
            cal_sum[half] = rows[:, half * LANE:(half + 1) * LANE]
            for par in range(2):
                spot = 8 + half * 4
                att_out[2 * t + par, spot:spot + 4, :] = cal_sum[half, pl.ds(par, 4, stride=2), :]


def obs_call(block_count, prefit, partials, attitude, position, calib, source, rng, knot, unit):
    blocks = block_count.shape[0]
    count = prefit.shape[0]
    pin = lambda value: pltpu.with_memory_space_constraint(value, pltpu.HBM)
    flat = lambda value: pin(value.reshape(1, -1))
    row = lambda kind: pltpu.VMEM((1, count), kind)
    listed = pltpu.SMEM((count // LANE + TURN + 8,), jnp.int32)
    return pl.pallas_call(
        obs_kernel,
        in_specs=[pl.BlockSpec(memory_space=pltpu.SMEM)] + [pl.BlockSpec(memory_space=pltpu.HBM)] * 9,
        out_specs=[pl.BlockSpec(memory_space=pltpu.VMEM)] * 2,
        out_shape=[
            jax.ShapeDtypeStruct((5, blocks * SRC_BLK), F32),
            jax.ShapeDtypeStruct((32, 16, LANE), F32),
        ],
        scratch_shapes=[
            row(F32), pltpu.VMEM((5, count), F32), pltpu.VMEM((4, count), F32), row(F32),
            pltpu.VMEM((3, count), F32), row(jnp.int32), row(jnp.int32), row(jnp.int32), row(jnp.int32),
            pltpu.VMEM((8, count), F32),
            pltpu.VMEM((blocks // GRP, 32, GRP, LANE), F32),
            pltpu.VMEM((8, blocks // GRP, GRP, LANE), F32),
            pltpu.VMEM((blocks, 8, LANE), F32),
            pltpu.VMEM((ATT_HI * 4, 256), F32),
            pltpu.VMEM((144, 256), F32),
            pltpu.VMEM((2, 8, LANE), F32),
            listed, listed, listed,
            pltpu.SemaphoreType.DMA((9,)),
        ],
        compiler_params=pltpu.CompilerParams(vmem_limit_bytes=VMEM_OBS),
    )(pin(block_count), flat(prefit), pin(partials), pin(attitude), flat(position), pin(calib), flat(source), flat(rng), flat(knot), flat(unit))


def hold_kernel(own_ref, inv_hbm, held_ref, sems):
    copies = []
    for part in range(8):
        rows = pl.ds(part * LANE, LANE)
        copies.append(pltpu.make_async_copy(inv_hbm.at[:, rows, :], held_ref.at[:, rows, :], sems.at[part]))
        copies[-1].start()
    for copy in copies:
        copy.wait()


def join_kernel(
    group_ref, own_ref, one_ref, two_ref, three_ref, inv_ref, decay_ref, send_ref, mul_ref, add_ref, rows_s
):
    total = own_ref[...] + one_ref[...] + two_ref[...] + three_ref[...]
    rows_s[...] = total
    group = group_ref[0]
    acc = jnp.zeros((8, 1024), F32)
    for half in range(2):
        for c in range(4):
            spot = half * 4 + c
            col = jnp.broadcast_to(total[spot:spot + 1, :], (LANE, LANE)).T
            first = c * 256 + half * LANE
            for s in range(LANE // 8):
                line = inv_ref[0, first + s * 8:first + s * 8 + 8, :]
                acc = acc + line * jnp.concatenate([col[s * 8:s * 8 + 8, :]] * 8, axis=1)
    flat = jnp.sum(acc, axis=0, keepdims=True)
    solved = jnp.concatenate([flat[:, c * 256:(c + 1) * 256] for c in range(4)], axis=0)
    decay = decay_ref[...]
    mul = decay
    add = jnp.sqrt(1.0 - decay * decay) * solved
    lane = lax.broadcasted_iota(jnp.int32, (4, 256), 1)
    shift = 1
    while shift < 256:
        inside = lane >= shift
        add = add + jnp.where(inside, mul * pltpu.roll(add, shift, 1), 0.0)
        mul = jnp.where(inside, mul * pltpu.roll(mul, shift, 1), mul)
        shift *= 2
    mul_ref[...] = mul
    add_ref[...] = add
    ends = jnp.where(
        lane[:, :LANE] < 64,
        jnp.broadcast_to(mul[:, 255:256], (4, LANE)),
        jnp.broadcast_to(add[:, 255:256], (4, LANE)),
    )
    out = jnp.concatenate([rows_s[pl.ds(8 + group, 1), :], rows_s[pl.ds(12 + group, 1), :], jnp.zeros((2, LANE), F32), ends], axis=0)
    send_ref[...] = jnp.broadcast_to(out[None], send_ref.shape)


def last_kernel(mine_ref, recv_ref, mul_ref, add_ref, att_ref, cal_ref):
    mine = mine_ref[0]
    lane = lax.broadcasted_iota(jnp.int32, (4, LANE), 1)
    state = jnp.zeros((4, LANE), F32)
    for r in range(31):
        ends = recv_ref[r, 4:8, :]
        turned = pltpu.roll(ends, 64, 1)
        longer = jnp.where(lane < 64, ends, turned) * state + jnp.where(lane < 64, turned, ends)
        state = jnp.where(r < mine, longer, state)
    att_ref[...] = add_ref[...] + mul_ref[...] * jnp.concatenate([state, state], axis=1)
    sums = [
        jnp.concatenate([recv_ref[2 * t, 0:2, :], recv_ref[2 * t + 1, 0:2, :]], axis=0)
        for t in range(9)
    ]
    matrix = [[None] * 3 for _ in range(3)]
    slot = 0
    for i in range(3):
        for j in range(i, 3):
            matrix[i][j] = sums[slot] + (1.0 if i == j else 0.0)
            matrix[j][i] = matrix[i][j]
            slot += 1
    answer = spd_solve(matrix, sums[6:9])
    rest = CAL_BASE - LANE
    for p in range(3):
        for par in range(2):
            first = par * CAL_BASE
            cal_ref[p:p + 1, first:first + LANE] = answer[p][2 * par:2 * par + 1, :]
            cal_ref[p:p + 1, first + LANE:first + CAL_BASE] = answer[p][2 * par + 1:2 * par + 2, :rest]


def on_device(
    prefit_resid, source_partials, attitude_partials, spline_position, calib_partials, obs_source,
    block_count, obs_range, obs_knot, obs_unit, given_inverse, knot_decay,
):
    update, packed = obs_call(
        block_count, prefit_resid, source_partials, attitude_partials, spline_position,
        calib_partials, obs_source, obs_range, obs_knot, obs_unit,
    )
    own = jnp.sum(lax.all_to_all(packed, "wide", 0, 0), axis=0)
    others = [
        lax.ppermute(own, "narrow", [(i, (i + shift) % 4) for i in range(4)]) for shift in (1, 2, 3)
    ]
    held = pl.pallas_call(
        hold_kernel,
        in_specs=[pl.BlockSpec(memory_space=pltpu.VMEM), pl.BlockSpec(memory_space=pltpu.HBM)],
        out_specs=pl.BlockSpec(memory_space=pltpu.VMEM),
        out_shape=jax.ShapeDtypeStruct(given_inverse.shape, F32),
        scratch_shapes=[pltpu.SemaphoreType.DMA((8,))],
        compiler_params=pltpu.CompilerParams(vmem_limit_bytes=8 * 1024 * 1024),
        cost_estimate=pl.CostEstimate(flops=0, bytes_accessed=8 * 1024 * 1024, transcendentals=0),
    )(own, pltpu.with_memory_space_constraint(given_inverse, pltpu.HBM))
    group = lax.axis_index("narrow").reshape(1).astype(jnp.int32)
    scalar = pl.BlockSpec(memory_space=pltpu.SMEM)
    vector = pl.BlockSpec(memory_space=pltpu.VMEM)
    small = jax.ShapeDtypeStruct((4, 256), F32)
    send, mul, add = pl.pallas_call(
        join_kernel,
        in_specs=[scalar] + [vector] * 6,
        out_shape=[jax.ShapeDtypeStruct((32, 8, LANE), F32), small, small],
        scratch_shapes=[
            pltpu.VMEM((16, LANE), F32),
        ],
        compiler_params=pltpu.CompilerParams(vmem_limit_bytes=16 * 1024 * 1024),
    )(group, own, *others, held, knot_decay)
    again = lax.all_to_all(send, "wide", 0, 0)
    mine = lax.axis_index("wide").reshape(1).astype(jnp.int32)
    att_update, cal_update = pl.pallas_call(
        last_kernel,
        in_specs=[scalar] + [vector] * 3,
        out_shape=[small, jax.ShapeDtypeStruct((3, 504), F32)],
        compiler_params=pltpu.CompilerParams(vmem_limit_bytes=16 * 1024 * 1024),
    )(mine, again, mul, add)
    return update, att_update, cal_update


def solution(mesh):
    both = ("wide", "narrow")
    placed = (
        P(both), P(None, both), P(None, both), P(both), P(None, both), P(both),
        P(both), P(both), P(both), P(both), P("wide", None, None), P(None, "wide"),
    )
    return jax.shard_map(
        on_device,
        mesh=mesh,
        in_specs=placed,
        out_specs=(P(None, both), P(None, "wide"), P(None, "narrow")),
        check_vma=False,
    )
```

```python
import jax
import jax.numpy as jnp
from jax import lax
from jax.experimental import pallas as pl
from jax.experimental.pallas import tpu as pltpu
from jax.sharding import PartitionSpec as P

SRC_BLK = 128
SLOT_BLK = 640
GRP = 8
TURN = 64
REST = 4
SPAN = 4
VMEM_OBS = 16 * 1024 * 1024
LANE = 128
ATT_BASE = 125
ATT_HI = 68
CAL_BASE = 252
F32 = jnp.float32
BF16 = jnp.bfloat16


def rounded(value):
    return value.astype(BF16).astype(F32)


def split3(value):
    top = rounded(value)
    rest = value - top
    mid = rounded(rest)
    return top, mid, rest - mid


def spd_solve(matrix, target):
    order = len(target)
    lower = [[None] * order for _ in range(order)]
    inv = [None] * order
    for col in range(order):
        pivot = matrix[col][col]
        for k in range(col):
            pivot = pivot - lower[col][k] * lower[col][k]
        inv[col] = 1.0 / jnp.sqrt(pivot)
        for row in range(col + 1, order):
            entry = matrix[row][col]
            for k in range(col):
                entry = entry - lower[row][k] * lower[col][k]
            lower[row][col] = entry * inv[col]
    forward = []
    for row in range(order):
        running = target[row]
        for k in range(row):
            running = running - lower[row][k] * forward[k]
        forward.append(running * inv[row])
    answer = [None] * order
    for row in reversed(range(order)):
        running = forward[row]
        for k in range(row + 1, order):
            running = running - lower[k][row] * answer[k]
        answer[row] = running * inv[row]
    return answer


NT = (((1,), (1,)), ((), ()))


def obs_kernel(
    count_ref, pre_hbm, par_hbm, att_hbm, pos_hbm, cal_hbm, src_hbm, rng_hbm, knot_hbm, unit_hbm,
    upd_ref, att_out,
    pre_ref, par_ref, att_ref, pos_ref, cal_ref, src_ref, rng_ref, knot_ref, unit_ref,
    tile_s, sums_s, upd_s, back_s,
    att_acc, cal_acc, cal_sum, start_s, live_s, block_s, sems,
):
    pairs = [
        (pre_hbm, pre_ref), (par_hbm, par_ref), (src_hbm, src_ref), (att_hbm, att_ref), (pos_hbm, pos_ref),
        (cal_hbm, cal_ref), (rng_hbm, rng_ref), (knot_hbm, knot_ref), (unit_hbm, unit_ref),
    ]
    copies = [pltpu.make_async_copy(src, dst, sems.at[i]) for i, (src, dst) in enumerate(pairs)]
    for copy in copies:
        copy.start()
    blocks = count_ref.shape[0]
    tiles = SLOT_BLK // LANE
    row8 = lax.broadcasted_iota(jnp.int32, (8, LANE), 0)
    row16 = lax.broadcasted_iota(jnp.int32, (16, LANE), 0)
    lane1 = lax.broadcasted_iota(jnp.int32, (1, LANE), 1)
    att_out[...] = jnp.zeros_like(att_out)

    def listing(block, spot):
        count = count_ref[block]
        for t in range(tiles):
            start_s[spot + t] = block * SLOT_BLK + t * LANE
            live_s[spot + t] = count - t * LANE
            block_s[spot + t] = block
        return spot + lax.shift_right_logical(count + (LANE - 1), 7)

    used = lax.fori_loop(0, blocks, listing, 0)
    for t in range(REST):
        start_s[used + t] = 0
        live_s[used + t] = 0
        block_s[used + t] = 0
    turns = lax.div(used, TURN)
    rests = lax.div(used - turns * TURN + (REST - 1), REST)

    for copy in copies[:3]:
        copy.wait()
    low8 = row8 < 4
    kk = jnp.bitwise_and(row8, 3)
    c0 = jnp.where(kk == 0, 1.0, jnp.where(kk == 1, 4.0, jnp.where(kk == 2, 1.0, 0.0))) / 6.0
    c1 = jnp.where(kk == 0, -3.0, jnp.where(kk == 2, 3.0, 0.0)) / 6.0
    c2 = jnp.where(kk == 0, 3.0, jnp.where(kk == 1, -6.0, jnp.where(kk == 2, 3.0, 0.0))) / 6.0
    c3 = jnp.where(kk == 0, -1.0, jnp.where(kk == 1, 3.0, jnp.where(kk == 2, -3.0, 1.0))) / 6.0
    quad16 = lax.shift_right_logical(row16, 2).astype(F32)
    mod16 = jnp.bitwise_and(row16, 7).astype(F32).astype(BF16)
    iota16 = row16.astype(F32).astype(BF16)
    zero16 = jnp.zeros((16, LANE), BF16)
    one16 = jnp.ones((16, LANE), BF16)

    def wide16(row):
        return jnp.broadcast_to(row, (16, LANE))

    def beside(left, right):
        return jnp.concatenate([left, right], axis=1)

    def one_hot(row16, count):
        return [jnp.where(iota16 + jnp.array(16 * t, BF16) == row16, one16, zero16) for t in range(count)]

    def source_tile(block, t):
        at = pl.ds(pl.multiple_of(block * SLOT_BLK + t * LANE, LANE), LANE)
        live = lane1 < count_ref[block] - t * LANE
        ids = jnp.where(live, src_ref[:, at], -1).astype(F32)
        par = par_ref[:, at]
        tile_s[0:5, at] = par
        tile_s[5:6, at] = pre_ref[:, at]
        tile_s[6:8, at] = par[0:2]
        tile = tile_s[:, at]
        turned = [tile] + [pltpu.roll(tile, 8 - d, 0) for d in (1, 2, 3)]
        pieces = []
        for d in (0, 2):
            both = jnp.concatenate([tile * turned[d], tile * turned[d + 1]], axis=0)
            pieces.append([part.astype(BF16) for part in split3(both)])
        return one_hot(wide16(ids).astype(BF16), 8), pieces

    def source_sums(accs):
        def spend_pair(group, pair, mine):
            unit = pair % 2
            block = group * GRP + 2 * pair
            for t in range(tiles):
                left_hot, left = source_tile(block, t)
                right_hot, right = source_tile(block + 1, t)
                rows = [beside(piece, zero16) for piece in left_hot]
                rows += [beside(zero16, piece) for piece in right_hot]
                stage = t % 2 if unit == pair else (t + 1) % 2
                pltpu.matmul_push_rhs(jnp.concatenate(rows, axis=0), stage, unit, transpose=True)
                for d in range(2):
                    for k in range(3):
                        pltpu.matmul_acc_lhs(mine[d], beside(left[d][k], right[d][k]), stage if d + k == 0 else None)

        def keep_pair(group, pair, mine):
            for d in range(2):
                sums = pltpu.matmul_pop(mine[d])
                for side in range(2):
                    sums_s[group, 16 * d:16 * d + 16, 2 * pair + side, :] = sums[:, side * LANE:(side + 1) * LANE]

        def group_sums(turn_at, _):
            for part in range(SPAN):
                for pair in range(GRP // 2):
                    spend_pair(turn_at * SPAN + part, pair, accs[part][pair])
            for part in range(SPAN):
                for pair in range(GRP // 2):
                    keep_pair(turn_at * SPAN + part, pair, accs[part][pair])
            return 0

        lax.fori_loop(0, blocks // (GRP * SPAN), group_sums, 0)

    pl.run_scoped(
        source_sums,
        [
            [[pltpu.ACC(pair % 2)((16, 256), F32) for _ in range(2)] for pair in range(GRP // 2)]
            for _ in range(SPAN)
        ],
    )

    matrix = [[None] * 5 for _ in range(5)]
    for i in range(5):
        for j in range(i, 5):
            apart = j - i
            spot = apart * 8 + i if apart < 4 else 20
            entry = sums_s[:, spot] + (1.0 if i == j else 0.0)
            matrix[i][j] = entry
            matrix[j][i] = entry
    answer = spd_solve(matrix, [sums_s[:, spot] for spot in (13, 21, 26, 19, 12)])
    for p in range(5):
        upd_s[p] = answer[p]
    upd_s[5] = jnp.full(upd_s.shape[1:], -1.0, F32)
    upd_s[6] = jnp.zeros(upd_s.shape[1:], F32)
    upd_s[7] = jnp.zeros(upd_s.shape[1:], F32)
    for block in range(blocks):
        mine = upd_s[:, block // GRP, block % GRP, :]
        back_s[block] = mine
        upd_ref[:, block * SRC_BLK:(block + 1) * SRC_BLK] = mine[0:5]
    for copy in copies[3:]:
        copy.wait()

    def tile_rows(entry):
        at = pl.ds(pl.multiple_of(start_s[entry], LANE), LANE)
        live = lane1 < live_s[entry]
        index = jnp.broadcast_to(src_ref[:, at], (8, LANE))
        picked = jnp.take_along_axis(back_s[block_s[entry]], index, axis=1, mode="promise_in_bounds")
        resid = jnp.where(live, -jnp.sum(picked * tile_s[:, at], axis=0, keepdims=True), 0.0)
        att4 = att_ref[:, at] * resid
        v8 = jnp.concatenate([att4, att4], axis=0)
        top8 = rounded(v8)
        rest8 = v8 - top8
        v16 = [jnp.concatenate([part, part], axis=0).astype(BF16) for part in (top8, rest8)]
        interval = (rng_ref[:, at] * 256 + knot_ref[:, at]).astype(F32)
        hi = jnp.floor((interval + 0.5) * (1.0 / ATT_BASE))
        lo = interval - hi * ATT_BASE
        hi16 = (wide16(hi) - quad16).astype(BF16)
        u = jnp.broadcast_to(pos_ref[:, at], (8, LANE))
        w8 = c0 + u * (c1 + u * (c2 + u * c3))
        top = rounded(w8)
        w8 = jnp.where(low8, top, w8 - top)
        los = [wide16(lo + float(k)).astype(BF16) for k in range(4)]
        ws = [wide16(w8[k:k + 1, :]).astype(BF16) for k in range(8)]
        unit = jnp.where(live, unit_ref[:, at], -1).astype(F32)
        uhi = jnp.floor((unit + 0.5) * (1.0 / CAL_BASE))
        ulo = unit - uhi * CAL_BASE
        same = wide16(uhi).astype(BF16) == mod16
        g8 = [jnp.broadcast_to(cal_ref[p:p + 1, at], (8, LANE)) for p in range(3)]
        r8 = jnp.broadcast_to(resid, (8, LANE))
        terms = [g8[i] * g8[j] for i in range(3) for j in range(i, 3)] + [g8[i] * r8 for i in range(3)]
        pieces = []
        for t in range(9):
            top = rounded(terms[t])
            both = jnp.concatenate([top, terms[t] - top], axis=0).astype(BF16)
            pieces.append(jnp.where(same, both, zero16))
        ul16 = wide16(ulo).astype(BF16)
        return v16, hi16, los, ws, pieces, ul16

    def knot_columns(los, ws):
        tops, lows = [], []
        for t in range(8):
            rows = iota16 + jnp.array(16 * t, BF16)
            top_part = zero16
            low_part = zero16
            for k in range(4):
                same = rows == los[k]
                top_part = jnp.where(same, ws[k], top_part)
                low_part = jnp.where(same, ws[4 + k], low_part)
            tops.append(top_part)
            lows.append(low_part)
        return jnp.concatenate(tops + lows, axis=0)

    def matmuls(att_accs, cal_accs):
        def spend(entry, unit):
            left, right = tile_rows(entry), tile_rows(entry + 1)
            pltpu.matmul_push_rhs(
                beside(knot_columns(left[2], left[3]), knot_columns(right[2], right[3])), 0, unit, transpose=True
            )
            for t in range(ATT_HI // 4):
                step = jnp.array(4 * t, BF16)
                same = [side[1] == step for side in (left, right)]
                for k in range(2):
                    rows = beside(jnp.where(same[0], left[0][k], zero16), jnp.where(same[1], right[0][k], zero16))
                    pltpu.matmul_acc_lhs(att_accs[unit][2 * t + k], rows, 0 if t + k == 0 else None)
            pltpu.matmul_push_rhs(
                beside(jnp.concatenate(one_hot(left[5], 16), axis=0), jnp.concatenate(one_hot(right[5], 16), axis=0)), 1, unit, transpose=True
            )
            for t in range(9):
                pltpu.matmul_acc_lhs(cal_accs[unit][t], beside(left[4][t], right[4][t]), 1 if t == 0 else None)

        def turn(turn_at, _):
            for part in range(TURN // 2):
                spend(turn_at * TURN + 2 * part, part % 2)
            return 0

        def rest(rest_at, _):
            for part in range(REST // 2):
                spend(turns * TURN + rest_at * REST + 2 * part, part % 2)
            return 0

        lax.fori_loop(0, turns, turn, 0)
        lax.fori_loop(0, rests, rest, 0)
        for t in range(ATT_HI // 4):
            parts = [pltpu.matmul_pop(att_accs[unit][2 * t + k]) for unit in range(2) for k in range(2)]
            att_acc[t * 16:(t + 1) * 16, :] = (parts[0] + parts[1]) + (parts[2] + parts[3])
        for t in range(9):
            cal_acc[t * 16:(t + 1) * 16, :] = pltpu.matmul_pop(cal_accs[0][t]) + pltpu.matmul_pop(cal_accs[1][t])

    pl.run_scoped(
        matmuls,
        [[pltpu.ACC(unit)((16, 256), F32) for _ in range(ATT_HI // 2)] for unit in range(2)],
        [[pltpu.ACC(unit)((16, 256), F32) for _ in range(9)] for unit in range(2)],
    )

    lane = lax.broadcasted_iota(jnp.int32, (4, LANE), 1)
    for h in range(ATT_HI):
        rows = att_acc[h * 4:(h + 1) * 4, :]
        piece = rows[:, :LANE] + rows[:, LANE:]
        where, shift = divmod(h * ATT_BASE, LANE)
        turned = pltpu.roll(piece, shift, 1) if shift else piece
        for part in range(2):
            spot = where + part
            if spot >= 64 or (part == 1 and shift == 0):
                continue
            keep = lane >= shift if part == 0 else lane < shift
            at = slice((spot % 2) * 4, (spot % 2) * 4 + 4)
            att_out[spot // 2, at, :] += jnp.where(keep, turned, 0.0)
    for t in range(9):
        rows = cal_acc[t * 16:(t + 1) * 16, :]
        rows = rows[0:8] + rows[8:16]
        for half in range(2):
            cal_sum[half] = rows[:, half * LANE:(half + 1) * LANE]
            for par in range(2):
                spot = 8 + half * 4
                att_out[2 * t + par, spot:spot + 4, :] = cal_sum[half, pl.ds(par, 4, stride=2), :]


def obs_call(block_count, prefit, partials, attitude, position, calib, source, rng, knot, unit):
    blocks = block_count.shape[0]
    count = prefit.shape[0]
    pin = lambda value: pltpu.with_memory_space_constraint(value, pltpu.HBM)
    flat = lambda value: pin(value.reshape(1, -1))
    row = lambda kind: pltpu.VMEM((1, count), kind)
    listed = pltpu.SMEM((count // LANE + TURN + 8,), jnp.int32)
    return pl.pallas_call(
        obs_kernel,
        in_specs=[pl.BlockSpec(memory_space=pltpu.SMEM)] + [pl.BlockSpec(memory_space=pltpu.HBM)] * 9,
        out_specs=[pl.BlockSpec(memory_space=pltpu.VMEM)] * 2,
        out_shape=[
            jax.ShapeDtypeStruct((5, blocks * SRC_BLK), F32),
            jax.ShapeDtypeStruct((32, 16, LANE), F32),
        ],
        scratch_shapes=[
            row(F32), pltpu.VMEM((5, count), F32), pltpu.VMEM((4, count), F32), row(F32),
            pltpu.VMEM((3, count), F32), row(jnp.int32), row(jnp.int32), row(jnp.int32), row(jnp.int32),
            pltpu.VMEM((8, count), F32),
            pltpu.VMEM((blocks // GRP, 32, GRP, LANE), F32),
            pltpu.VMEM((8, blocks // GRP, GRP, LANE), F32),
            pltpu.VMEM((blocks, 8, LANE), F32),
            pltpu.VMEM((ATT_HI * 4, 256), F32),
            pltpu.VMEM((144, 256), F32),
            pltpu.VMEM((2, 8, LANE), F32),
            listed, listed, listed,
            pltpu.SemaphoreType.DMA((9,)),
        ],
        compiler_params=pltpu.CompilerParams(vmem_limit_bytes=VMEM_OBS),
    )(pin(block_count), flat(prefit), pin(partials), pin(attitude), flat(position), pin(calib), flat(source), flat(rng), flat(knot), flat(unit))


def hold_kernel(own_ref, inv_hbm, held_ref, sems):
    copies = []
    for part in range(8):
        rows = pl.ds(part * LANE, LANE)
        copies.append(pltpu.make_async_copy(inv_hbm.at[:, rows, :], held_ref.at[:, rows, :], sems.at[part]))
        copies[-1].start()
    for copy in copies:
        copy.wait()


def join_kernel(
    group_ref, own_ref, one_ref, two_ref, three_ref, inv_ref, decay_ref, send_ref, mul_ref, add_ref, rows_s
):
    total = own_ref[...] + one_ref[...] + two_ref[...] + three_ref[...]
    rows_s[...] = total
    group = group_ref[0]
    acc = jnp.zeros((8, 1024), F32)
    for half in range(2):
        for c in range(4):
            spot = half * 4 + c
            col = jnp.broadcast_to(total[spot:spot + 1, :], (LANE, LANE)).T
            first = c * 256 + half * LANE
            for s in range(LANE // 8):
                line = inv_ref[0, first + s * 8:first + s * 8 + 8, :]
                acc = acc + line * jnp.concatenate([col[s * 8:s * 8 + 8, :]] * 8, axis=1)
    flat = jnp.sum(acc, axis=0, keepdims=True)
    solved = jnp.concatenate([flat[:, c * 256:(c + 1) * 256] for c in range(4)], axis=0)
    decay = decay_ref[...]
    mul = decay
    add = jnp.sqrt(1.0 - decay * decay) * solved
    lane = lax.broadcasted_iota(jnp.int32, (4, 256), 1)
    shift = 1
    while shift < 256:
        inside = lane >= shift
        add = add + jnp.where(inside, mul * pltpu.roll(add, shift, 1), 0.0)
        mul = jnp.where(inside, mul * pltpu.roll(mul, shift, 1), mul)
        shift *= 2
    mul_ref[...] = mul
    add_ref[...] = add
    ends = jnp.where(
        lane[:, :LANE] < 64,
        jnp.broadcast_to(mul[:, 255:256], (4, LANE)),
        jnp.broadcast_to(add[:, 255:256], (4, LANE)),
    )
    out = jnp.concatenate([rows_s[pl.ds(8 + group, 1), :], rows_s[pl.ds(12 + group, 1), :], jnp.zeros((2, LANE), F32), ends], axis=0)
    send_ref[...] = jnp.broadcast_to(out[None], send_ref.shape)


def last_kernel(mine_ref, recv_ref, mul_ref, add_ref, att_ref, cal_ref):
    mine = mine_ref[0]
    lane = lax.broadcasted_iota(jnp.int32, (4, LANE), 1)
    state = jnp.zeros((4, LANE), F32)
    for r in range(31):
        ends = recv_ref[r, 4:8, :]
        turned = pltpu.roll(ends, 64, 1)
        longer = jnp.where(lane < 64, ends, turned) * state + jnp.where(lane < 64, turned, ends)
        state = jnp.where(r < mine, longer, state)
    att_ref[...] = add_ref[...] + mul_ref[...] * jnp.concatenate([state, state], axis=1)
    sums = [
        jnp.concatenate([recv_ref[2 * t, 0:2, :], recv_ref[2 * t + 1, 0:2, :]], axis=0)
        for t in range(9)
    ]
    matrix = [[None] * 3 for _ in range(3)]
    slot = 0
    for i in range(3):
        for j in range(i, 3):
            matrix[i][j] = sums[slot] + (1.0 if i == j else 0.0)
            matrix[j][i] = matrix[i][j]
            slot += 1
    answer = spd_solve(matrix, sums[6:9])
    rest = CAL_BASE - LANE
    for p in range(3):
        for par in range(2):
            first = par * CAL_BASE
            cal_ref[p:p + 1, first:first + LANE] = answer[p][2 * par:2 * par + 1, :]
            cal_ref[p:p + 1, first + LANE:first + CAL_BASE] = answer[p][2 * par + 1:2 * par + 2, :rest]


def on_device(
    prefit_resid, source_partials, attitude_partials, spline_position, calib_partials, obs_source,
    block_count, obs_range, obs_knot, obs_unit, given_inverse, knot_decay,
):
    update, packed = obs_call(
        block_count, prefit_resid, source_partials, attitude_partials, spline_position,
        calib_partials, obs_source, obs_range, obs_knot, obs_unit,
    )
    own = jnp.sum(lax.all_to_all(packed, "wide", 0, 0), axis=0)
    others = [
        lax.ppermute(own, "narrow", [(i, (i + shift) % 4) for i in range(4)]) for shift in (1, 2, 3)
    ]
    held = pl.pallas_call(
        hold_kernel,
        in_specs=[pl.BlockSpec(memory_space=pltpu.VMEM), pl.BlockSpec(memory_space=pltpu.HBM)],
        out_specs=pl.BlockSpec(memory_space=pltpu.VMEM),
        out_shape=jax.ShapeDtypeStruct(given_inverse.shape, F32),
        scratch_shapes=[pltpu.SemaphoreType.DMA((8,))],
        compiler_params=pltpu.CompilerParams(vmem_limit_bytes=8 * 1024 * 1024),
        cost_estimate=pl.CostEstimate(flops=0, bytes_accessed=8 * 1024 * 1024, transcendentals=0),
    )(own, pltpu.with_memory_space_constraint(given_inverse, pltpu.HBM))
    group = lax.axis_index("narrow").reshape(1).astype(jnp.int32)
    scalar = pl.BlockSpec(memory_space=pltpu.SMEM)
    vector = pl.BlockSpec(memory_space=pltpu.VMEM)
    small = jax.ShapeDtypeStruct((4, 256), F32)
    send, mul, add = pl.pallas_call(
        join_kernel,
        in_specs=[scalar] + [vector] * 6,
        out_shape=[jax.ShapeDtypeStruct((32, 8, LANE), F32), small, small],
        scratch_shapes=[
            pltpu.VMEM((16, LANE), F32),
        ],
        compiler_params=pltpu.CompilerParams(vmem_limit_bytes=16 * 1024 * 1024),
    )(group, own, *others, held, knot_decay)
    again = lax.all_to_all(send, "wide", 0, 0)
    mine = lax.axis_index("wide").reshape(1).astype(jnp.int32)
    att_update, cal_update = pl.pallas_call(
        last_kernel,
        in_specs=[scalar] + [vector] * 3,
        out_shape=[small, jax.ShapeDtypeStruct((3, 504), F32)],
        compiler_params=pltpu.CompilerParams(vmem_limit_bytes=16 * 1024 * 1024),
    )(mine, again, mul, add)
    return update, att_update, cal_update


def solution(mesh):
    both = ("wide", "narrow")
    placed = (
        P(both), P(None, both), P(None, both), P(both), P(None, both), P(both),
        P(both), P(both), P(both), P(both), P("wide", None, None), P(None, "wide"),
    )
    return jax.shard_map(
        on_device,
        mesh=mesh,
        in_specs=placed,
        out_specs=(P(None, both), P(None, "wide"), P(None, "narrow")),
        check_vma=False,
    )
```
